128 devices in a mesh: ctx: 32 (over z, x, y_lo), tp: 4 (over y_hi, core).
Axes of the slice: x: 4, y: 4 (y_hi: 2, y_lo: 2; y = y_hi * 2 + y_lo), z: 4, core: 2. Of those that a mesh axis runs over, the one named last changes fastest.
Arguments:
- signal: bfloat16 [4096, 2048], P('ctx', 'tp'), may hold values from -6 to 6
- gate: bfloat16 [4096, 2048], P('ctx', 'tp'), may hold values from -6 to 6
- filt: bfloat16 [4096, 2048], P('ctx', 'tp'), may hold values from -0.25 to 0.25
- bias: float32 [2048], P('tp'), may hold values from -2 to 2
- doc_ids: int32 [4096], replicated, may hold values from 0 to 3, never falling along the last dimension, each value on 1 to 3840 neighbouring positions
- block_perm: int32 [64], replicated, may hold values from 0 to 63, each once
- out_weight: bfloat16 [2048, 2048], P('tp'), may hold values from -0.125 to 0.125
Outputs:
- mixed: bfloat16 [4096, 2048], P('ctx', 'tp')
The draws below stay inside these ranges and needn't reach their ends.
Inputs may be any that keep to these rules, and one draw needn't show every extreme that they name: `doc_ids`: ids never fall along the sequence; each document is a run of 1 to 3840 positions, one exactly 3840. `block_perm`: each block number once.
All inputs are finite; a program needn't handle non-finite values.
Results may differ from the reference program's by a relative error of at most 0.012.
Values may be sent and summed in bfloat16 or wider, within the bound.
No kernel may reach another device: no remote copies, remote signals or barrier semaphores. Data moves between devices by JAX's collectives and lax.ppermute only.
A program may use at most 64 MiB of HBM per device.

```python
import math
import jax
import jax.numpy as jnp
import numpy as np
from jax import lax

W = 2048
SPAN = 64
DOCS = 4
SEQ = 4096
DOC_MOST = 3840
N_CTX = 32


def level_of(key, shape, cuts, least, high):
    def one(axis_at, shards_of):
        draws = jax.random.uniform(jax.random.fold_in(jax.random.fold_in(key, 6), axis_at), (shards_of,), jnp.float32, least / len(cuts), high / len(cuts))
        return jnp.repeat(jnp.exp(draws), shape[axis_at] // shards_of).reshape((-1,) + (1,) * (len(shape) - axis_at - 1))

    level = one(*cuts[0])
    for cut in cuts[1:]:
        level = level * one(*cut)
    return level


def split_up(count, total, reach, skew):
    weights = [(1 << 20) // math.isqrt(standing ** skew) + 1 for standing in range(2, count + 1)]
    spare, counts = total - reach - (count - 1), [1] * (count - 1)
    while spare > 0:
        candidates = [i for i in range(count - 1) if counts[i] < reach]
        pool, remaining = sum([weights[i] for i in candidates]), spare
        for i in candidates:
            addition = min(reach - counts[i], max(1, remaining * weights[i] // pool), spare)
            counts[i] = counts[i] + addition
            spare = spare - addition
    return np.array([reach] + counts)


def uneven_parts(own_key, number_of, total, limit, slope):
    if number_of == 2:
        one = jax.random.randint(own_key, (), max(1, total - limit), min(limit, total - 1) + 1)
        return jnp.stack([one, total - one])
    tallies = jnp.asarray(split_up(number_of, total, limit, slope), jnp.int32)
    twos = (number_of - 1) // 2
    giver, receiver = tallies[1:1 + 2 * twos:2], tallies[2:2 + 2 * twos:2]
    slack = jnp.minimum(giver - 1, limit - receiver)
    shifted = jax.random.randint(jax.random.fold_in(own_key, 1), (twos,), 0, 1 << 20) % (slack + 1)
    tallies = tallies.at[1:1 + 2 * twos:2].set(giver - shifted).at[2:2 + 2 * twos:2].set(receiver + shifted)
    return tallies[jax.random.permutation(jax.random.fold_in(own_key, 2), number_of)]


def normal_values(stream_key, dims, deviation, most, pieces=(), held_as=jnp.bfloat16):
    loudness = level_of(stream_key, dims, pieces, -0.22, 0.18) if pieces else 1.0
    drawn = jax.random.normal(stream_key, dims, jnp.float32) * deviation * loudness
    return jnp.minimum(jnp.maximum(drawn, -most), most).astype(held_as)


def setup_inputs(seed: int = 0) -> dict:
    splits = jax.random.split(jax.random.key(seed), 8)
    return {
        "signal": normal_values(splits[0], (SEQ, W), 1.0, 6.0, ((0, 32), (1, 4))),
        "gate": normal_values(splits[1], (SEQ, W), 1.0, 6.0, ((0, 32), (1, 4))),
        "filt": normal_values(splits[2], (SEQ, W), (8 * SPAN) ** -0.5, 0.25, ((0, 32), (1, 4))),
        "bias": normal_values(splits[3], (W,), 0.5, 2.0, ((0, 4),), jnp.float32),
        "doc_ids": jnp.searchsorted(jnp.cumsum(uneven_parts(splits[4], DOCS, SEQ, DOC_MOST, 0)), jnp.arange(SEQ), side="right").astype(jnp.int32),
        "block_perm": jax.random.permutation(splits[5], 2 * N_CTX).astype(jnp.int32),
        "out_weight": normal_values(splits[6], (W, W), W ** -0.5, 0.125, ((0, 4),)),
    }


def reference(signal, gate, filt, bias, doc_ids, block_perm, out_weight):
    blocks = 2 * N_CTX
    natural_x = jnp.zeros((blocks, SPAN, W), signal.dtype).at[block_perm].set(signal.reshape(blocks, SPAN, W)).reshape(SEQ, W)
    natural_g = jnp.zeros((blocks, SPAN, W), gate.dtype).at[block_perm].set(gate.reshape(blocks, SPAN, W)).reshape(SEQ, W)
    source = natural_x.astype(jnp.float32)
    kernel_spec = jnp.fft.rfft(filt.astype(jnp.float32), n=2 * SEQ, axis=0)

    def add_document(doc, running):
        member = (doc_ids == doc).astype(jnp.float32)[:, None]
        spec = jnp.fft.rfft(source * member, n=2 * SEQ, axis=0)
        conv = jnp.fft.irfft(kernel_spec * spec, n=2 * SEQ, axis=0)[:SEQ]
        return running + conv * member

    conv = lax.fori_loop(0, DOCS, add_document, jnp.zeros((SEQ, W), jnp.float32))
    gated = (natural_g.astype(jnp.float32) * (conv + bias[None, :] * source)).astype(jnp.bfloat16)
    mixed = jnp.dot(gated, out_weight, preferred_element_type=jnp.float32).astype(jnp.bfloat16)
    return mixed.reshape(blocks, SPAN, W)[block_perm].reshape(SEQ, W)
```

```python
import jax
import jax.numpy as jnp
from jax import lax
from jax.sharding import PartitionSpec as P

SPAN = 64
DOC_COUNT = 4


def skew_blocks(a, fill):
    chans, blocks, span = a.shape
    a_ext = jnp.concatenate([a, jnp.full_like(a, fill)], axis=1)
    tiled = jnp.broadcast_to(a_ext[:, None], (chans, blocks, 2 * blocks, span))
    tiled = tiled.reshape(chans, blocks * 2 * blocks, span)[:, : blocks * (2 * blocks - 1)]
    return tiled.reshape(chans, blocks, 2 * blocks - 1, span)[:, :, :blocks]


def block_conv(x_cm, f_cm, doc_ids):
    chans, seq = x_cm.shape
    span = SPAN
    blocks = seq // span
    width = seq + span
    f_ext = jnp.pad(f_cm, ((0, 0), (0, span)))
    tt = jnp.broadcast_to(f_ext[:, None, :], (chans, span, width)).reshape(chans, span * width)
    tt = tt[:, : span * (width - 1)].reshape(chans, span, width - 1)[:, :, :seq]
    tt = tt.reshape(chans, span, blocks, span)
    xb = x_cm.reshape(chans, blocks, span)
    src = skew_blocks(xb, 0)
    docb = doc_ids.reshape(blocks, span)
    lead = docb[:, 0]
    src_doc = skew_blocks(docb[None], -1)[0]
    keep = src_doc == lead[None, :, None]
    src = jnp.where(keep[None], src, jnp.zeros_like(src))
    lead_part = jnp.einsum("cjdi,cdtj->cit", tt, src, preferred_element_type=jnp.float32)
    row_doc = docb.T
    lead_rows = row_doc == lead[None, :]
    out = jnp.where(lead_rows[None], lead_part, 0.0)
    near = tt[:, :, 0, :]
    xt = jnp.swapaxes(xb, 1, 2)
    for doc in range(DOC_COUNT):
        member = (docb.T == doc)
        part = jnp.einsum(
            "cji,cjt->cit",
            near,
            jnp.where(member[None], xt, jnp.zeros_like(xt)),
            preferred_element_type=jnp.float32,
        )
        rows = member & (lead[None, :] != doc)
        out = out + jnp.where(rows[None], part, 0.0)
    return jnp.swapaxes(out, 1, 2).reshape(chans, seq)


def body(signal, gate, filt, bias, doc_ids, block_perm, out_weight):
    span = SPAN
    rows, chans = signal.shape
    blocks = block_perm.shape[0]
    seq = blocks * span
    n_ctx = seq // rows
    per_dev = chans // n_ctx
    ctx_index = lax.axis_index("ctx")

    def to_channel_major(a):
        return lax.all_to_all(a, "ctx", 1, 0, tiled=True).T

    inverse = jnp.zeros((blocks,), jnp.int32).at[block_perm].set(jnp.arange(blocks, dtype=jnp.int32))

    def slots_to_natural(a):
        return jnp.take(a.reshape(per_dev, blocks, span), inverse, axis=1).reshape(per_dev, seq)

    x_cm = slots_to_natural(to_channel_major(signal))
    g_cm = slots_to_natural(to_channel_major(gate))
    f_cm = to_channel_major(filt)
    bias_cm = lax.dynamic_slice_in_dim(bias, ctx_index * per_dev, per_dev)
    group = 4
    conv = lax.map(
        lambda xf: block_conv(xf[0], xf[1], doc_ids),
        (x_cm.reshape(per_dev // group, group, seq), f_cm.reshape(per_dev // group, group, seq)),
    ).reshape(per_dev, seq)
    gated = (
        g_cm.astype(jnp.float32) * (conv + bias_cm[:, None] * x_cm.astype(jnp.float32))
    ).astype(jnp.bfloat16)
    gated_slots = jnp.take(gated.reshape(per_dev, blocks, span), block_perm, axis=1)
    gated_slots = gated_slots.reshape(per_dev, seq).T
    gated_local = lax.all_to_all(gated_slots, "ctx", 0, 1, tiled=True)
    partial_value = jnp.dot(gated_local, out_weight, preferred_element_type=jnp.float32)
    return lax.psum_scatter(partial_value, "tp", scatter_dimension=1, tiled=True).astype(
        jnp.bfloat16
    )


def solution(mesh):
    return jax.shard_map(
        body,
        mesh=mesh,
        in_specs=(P("ctx", "tp"), P("ctx", "tp"), P("ctx", "tp"), P("tp"), P(), P(), P("tp", None)),
        out_specs=P("ctx", "tp"),
        check_vma=False,
    )
```

```python
import jax
import jax.numpy as jnp
from jax import lax
from jax.experimental import pallas as pl
from jax.experimental.pallas import tpu as pltpu
from jax.sharding import PartitionSpec as P

SPAN = 64
DOC_COUNT = 4


def conv_kernel(f_ref, x_ref, doc_ref, mz_ref, y_ref):
    blocks, span = x_ref.shape[1], x_ref.shape[2]
    seq = blocks * span
    width = f_ref.shape[2]
    lanes = 2 * span
    fb = jnp.broadcast_to(f_ref[0].astype(jnp.float32), (span, width))
    tt = pltpu.roll(fb, 0, 1, stride=1, stride_axis=0)[:, :seq].astype(jnp.bfloat16)
    x = x_ref[0]
    docs = doc_ref[...]
    lead = docs[:, 0:1]
    last = docs[:, span - 1 : span]
    zero = jnp.zeros_like(x)
    x_lead = jnp.where(docs == lead, x, zero)
    x_last = jnp.where((docs == last) & (docs != lead), x, zero)
    z_lead = jnp.dot(x_lead, tt, preferred_element_type=jnp.float32)
    z_last = jnp.dot(x_last, tt, preferred_element_type=jnp.float32)
    zm = z_lead * mz_ref[0] + z_last * mz_ref[1]
    acc = zm[:, :lanes]
    for pair in range(1, seq // lanes):
        acc = acc + pltpu.roll(zm[:, pair * lanes : (pair + 1) * lanes], 2 * pair, 0)
    y = acc[:, :span] + pltpu.roll(acc[:, span:], 1, 0)
    near = tt[:, :span]
    planes = jnp.concatenate([jnp.where(docs == doc, x, zero) for doc in range(DOC_COUNT)], axis=0)
    local = jnp.dot(planes, near, preferred_element_type=jnp.float32)
    for doc in range(DOC_COUNT):
        y = y + jnp.where(docs == doc, local[doc * blocks : (doc + 1) * blocks], 0.0)
    y_ref[0] = y


def pallas_conv(x_cm, f_cm, doc_ids):
    chans, seq = x_cm.shape
    span = SPAN
    blocks = seq // span
    width = seq + 2 * span
    f_ext = jnp.pad(f_cm, ((0, 0), (0, width - seq))).reshape(chans, 1, width)
    xb = x_cm.reshape(chans, blocks, span)
    docb = doc_ids.reshape(blocks, span)
    ends = jnp.sum(doc_ids[None, None, :] <= jnp.stack([docb[:, 0], docb[:, -1]])[:, :, None], axis=2)
    rel = lax.broadcasted_iota(jnp.int32, (blocks, seq), 1)
    pos = rel + span * lax.broadcasted_iota(jnp.int32, (blocks, seq), 0)
    mz = ((rel >= span)[None] & (pos[None] < ends[:, :, None])).astype(jnp.float32)
    out = pl.pallas_call(
        conv_kernel,
        grid=(chans,),
        in_specs=[
            pl.BlockSpec((1, 1, width), lambda c: (c, 0, 0)),
            pl.BlockSpec((1, blocks, span), lambda c: (c, 0, 0)),
            pl.BlockSpec((blocks, span), lambda c: (0, 0)),
            pl.BlockSpec((2, blocks, seq), lambda c: (0, 0, 0)),
        ],
        out_specs=pl.BlockSpec((1, blocks, span), lambda c: (c, 0, 0)),
        out_shape=jax.ShapeDtypeStruct((chans, blocks, span), jnp.float32),
    )(f_ext, xb, docb, mz)
    return out.reshape(chans, seq)


def body(signal, gate, filt, bias, doc_ids, block_perm, out_weight):
    span = SPAN
    rows, chans = signal.shape
    blocks = block_perm.shape[0]
    seq = blocks * span
    n_ctx = seq // rows
    per_dev = chans // n_ctx
    ctx_index = lax.axis_index("ctx")

    def to_channel_major(a):
        return lax.all_to_all(a, "ctx", 1, 0, tiled=True).T

    inverse = jnp.zeros((blocks,), jnp.int32).at[block_perm].set(jnp.arange(blocks, dtype=jnp.int32))

    def slots_to_natural(a):
        return jnp.take(a.reshape(per_dev, blocks, span), inverse, axis=1).reshape(per_dev, seq)

    x_cm = slots_to_natural(to_channel_major(signal))
    g_cm = slots_to_natural(to_channel_major(gate))
    f_cm = to_channel_major(filt)
    bias_cm = lax.dynamic_slice_in_dim(bias, ctx_index * per_dev, per_dev)
    conv = pallas_conv(x_cm, f_cm, doc_ids)
    gated = (
        g_cm.astype(jnp.float32) * (conv + bias_cm[:, None] * x_cm.astype(jnp.float32))
    ).astype(jnp.bfloat16)
    gated_slots = jnp.take(gated.reshape(per_dev, blocks, span), block_perm, axis=1)
    gated_slots = gated_slots.reshape(per_dev, seq).T
    gated_local = lax.all_to_all(gated_slots, "ctx", 0, 1, tiled=True)
    partial_value = jnp.dot(gated_local, out_weight, preferred_element_type=jnp.float32)
    return lax.psum_scatter(partial_value, "tp", scatter_dimension=1, tiled=True).astype(
        jnp.bfloat16
    )


def solution(mesh):
    return jax.shard_map(
        body,
        mesh=mesh,
        in_specs=(P("ctx", "tp"), P("ctx", "tp"), P("ctx", "tp"), P("tp"), P(), P(), P("tp", None)),
        out_specs=P("ctx", "tp"),
        check_vma=False,
    )
```

```python
import jax
import jax.numpy as jnp
from jax import lax
from jax.experimental import pallas as pl
from jax.experimental.pallas import tpu as pltpu
from jax.sharding import PartitionSpec as P

SPAN = 64
DOC_COUNT = 4


def conv_kernel(f_ref, x_ref, doc_ref, mz_ref, y_ref):
    blocks, span = x_ref.shape[1], x_ref.shape[2]
    seq = blocks * span
    width = f_ref.shape[2]
    lanes = 2 * span
    fb = jnp.broadcast_to(f_ref[0].astype(jnp.float32), (span, width))
    tt = pltpu.roll(fb, 0, 1, stride=1, stride_axis=0)[:, :seq].astype(jnp.bfloat16)
    x = x_ref[0]
    docs = doc_ref[...]
    lead = docs[:, 0:1]
    last = docs[:, span - 1 : span]
    zero = jnp.zeros_like(x)
    x_lead = jnp.where(docs == lead, x, zero)
    x_last = jnp.where((docs == last) & (docs != lead), x, zero)
    z_lead = jnp.dot(x_lead, tt, preferred_element_type=jnp.float32)
    z_last = jnp.dot(x_last, tt, preferred_element_type=jnp.float32)
    zm = z_lead * mz_ref[0] + z_last * mz_ref[1]
    acc = zm[:, :lanes]
    for pair in range(1, seq // lanes):
        acc = acc + pltpu.roll(zm[:, pair * lanes : (pair + 1) * lanes], 2 * pair, 0)
    y = acc[:, :span] + pltpu.roll(acc[:, span:], 1, 0)
    near = tt[:, :span]
    planes = jnp.concatenate([jnp.where(docs == doc, x, zero) for doc in range(DOC_COUNT)], axis=0)
    local = jnp.dot(planes, near, preferred_element_type=jnp.float32)
    for doc in range(DOC_COUNT):
        y = y + jnp.where(docs == doc, local[doc * blocks : (doc + 1) * blocks], 0.0)
    y_ref[0] = y


def pallas_conv(x_cm, f_cm, doc_ids):
    chans, seq = x_cm.shape
    span = SPAN
    blocks = seq // span
    width = seq + 2 * span
    f_ext = jnp.pad(f_cm, ((0, 0), (0, width - seq))).reshape(chans, 1, width)
    xb = x_cm.reshape(chans, blocks, span)
    docb = doc_ids.reshape(blocks, span)
    ends = jnp.sum(doc_ids[None, None, :] <= jnp.stack([docb[:, 0], docb[:, -1]])[:, :, None], axis=2)
    rel = lax.broadcasted_iota(jnp.int32, (blocks, seq), 1)
    pos = rel + span * lax.broadcasted_iota(jnp.int32, (blocks, seq), 0)
    mz = ((rel >= span)[None] & (pos[None] < ends[:, :, None])).astype(jnp.float32)
    out = pl.pallas_call(
        conv_kernel,
        grid=(chans,),
        in_specs=[
            pl.BlockSpec((1, 1, width), lambda c: (c, 0, 0)),
            pl.BlockSpec((1, blocks, span), lambda c: (c, 0, 0)),
            pl.BlockSpec((blocks, span), lambda c: (0, 0)),
            pl.BlockSpec((2, blocks, seq), lambda c: (0, 0, 0)),
        ],
        out_specs=pl.BlockSpec((1, blocks, span), lambda c: (c, 0, 0)),
        out_shape=jax.ShapeDtypeStruct((chans, blocks, span), jnp.float32),
    )(f_ext, xb, docb, mz)
    return out.reshape(chans, seq)


def body(signal, gate, filt, bias, doc_ids, block_perm, out_weight):
    span = SPAN
    rows, chans = signal.shape
    blocks = block_perm.shape[0]
    seq = blocks * span
    n_ctx = seq // rows
    per_dev = chans // n_ctx
    ctx_index = lax.axis_index("ctx")

    inverse = jnp.zeros((blocks,), jnp.int32).at[block_perm].set(jnp.arange(blocks, dtype=jnp.int32))

    def slots_to_natural(a):
        return jnp.take(a.reshape(per_dev, blocks, span), inverse, axis=1).reshape(per_dev, seq)

    packed = jnp.stack(
        [a.reshape(rows, n_ctx, per_dev) for a in (signal, gate, filt)], axis=2
    ).reshape(rows, n_ctx * 3 * per_dev)
    arrived = lax.all_to_all(packed, "ctx", 1, 0, tiled=True).T
    x_cm = slots_to_natural(arrived[:per_dev])
    g_cm = slots_to_natural(arrived[per_dev : 2 * per_dev])
    f_cm = arrived[2 * per_dev :]
    bias_cm = lax.dynamic_slice_in_dim(bias, ctx_index * per_dev, per_dev)
    conv = pallas_conv(x_cm, f_cm, doc_ids)
    gated = (
        g_cm.astype(jnp.float32) * (conv + bias_cm[:, None] * x_cm.astype(jnp.float32))
    ).astype(jnp.bfloat16)
    gated_slots = jnp.take(gated.reshape(per_dev, blocks, span), block_perm, axis=1)
    gated_slots = gated_slots.reshape(per_dev, seq).T
    gated_local = lax.all_to_all(gated_slots, "ctx", 0, 1, tiled=True)
    tp_index = lax.axis_index("tp")
    n_tp = out_weight.shape[1] // chans
    high, core = tp_index // 2, tp_index % 2
    half = out_weight.shape[1] // 2
    w_other = lax.dynamic_slice_in_dim(out_weight, (1 - high) * half, half, axis=1)
    p_other = jnp.dot(gated_local, w_other, preferred_element_type=jnp.float32)
    recv_high = lax.ppermute(p_other, "tp", [(i, i ^ 2) for i in range(n_tp)])
    w_mine = lax.dynamic_slice_in_dim(out_weight, high * half, half, axis=1)
    p_mine = jnp.dot(gated_local, w_mine, preferred_element_type=jnp.float32) + recv_high
    send_core = lax.dynamic_slice_in_dim(p_mine, (1 - core) * chans, chans, axis=1)
    keep_core = lax.dynamic_slice_in_dim(p_mine, core * chans, chans, axis=1)
    recv_core = lax.ppermute(send_core, "tp", [(i, i ^ 1) for i in range(n_tp)])
    return (keep_core + recv_core).astype(jnp.bfloat16)


def solution(mesh):
    return jax.shard_map(
        body,
        mesh=mesh,
        in_specs=(P("ctx", "tp"), P("ctx", "tp"), P("ctx", "tp"), P("tp"), P(), P(), P("tp", None)),
        out_specs=P("ctx", "tp"),
        check_vma=False,
    )
```

```python
import jax
import jax.numpy as jnp
from jax import lax
from jax.experimental import pallas as pl
from jax.experimental.pallas import tpu as pltpu
from jax.sharding import PartitionSpec as P

SPAN = 64
DOC_COUNT = 4


def conv_kernel(f_ref, x_ref, doc_ref, mz_ref, y_ref):
    blocks, span = x_ref.shape[1], x_ref.shape[2]
    seq = blocks * span
    width = f_ref.shape[2]
    lanes = 2 * span
    fb = jnp.broadcast_to(f_ref[0].astype(jnp.float32), (span, width))
    tt = pltpu.roll(fb, 0, 1, stride=1, stride_axis=0)[:, :seq].astype(jnp.bfloat16)
    x = x_ref[0]
    docs = doc_ref[...]
    lead = docs[:, 0:1]
    last = docs[:, span - 1 : span]
    zero = jnp.zeros_like(x)
    x_lead = jnp.where(docs == lead, x, zero)
    x_last = jnp.where((docs == last) & (docs != lead), x, zero)
    z_lead = jnp.dot(x_lead, tt, preferred_element_type=jnp.float32)
    z_last = jnp.dot(x_last, tt, preferred_element_type=jnp.float32)
    zm = z_lead * mz_ref[0] + z_last * mz_ref[1]
    acc = zm[:, :lanes]
    for pair in range(1, seq // lanes):
        acc = acc + pltpu.roll(zm[:, pair * lanes : (pair + 1) * lanes], 2 * pair, 0)
    y = acc[:, :span] + pltpu.roll(acc[:, span:], 1, 0)
    near = tt[:, :span]
    planes = jnp.concatenate([jnp.where(docs == doc, x, zero) for doc in range(DOC_COUNT)], axis=0)
    local = jnp.dot(planes, near, preferred_element_type=jnp.float32)
    for doc in range(DOC_COUNT):
        y = y + jnp.where(docs == doc, local[doc * blocks : (doc + 1) * blocks], 0.0)
    y_ref[0] = y


def pallas_conv(x_cm, f_cm, doc_ids):
    chans, seq = x_cm.shape
    span = SPAN
    blocks = seq // span
    width = seq + 2 * span
    f_ext = jnp.pad(f_cm, ((0, 0), (0, width - seq))).reshape(chans, 1, width)
    xb = x_cm.reshape(chans, blocks, span)
    docb = doc_ids.reshape(blocks, span)
    ends = jnp.sum(doc_ids[None, None, :] <= jnp.stack([docb[:, 0], docb[:, -1]])[:, :, None], axis=2)
    rel = lax.broadcasted_iota(jnp.int32, (blocks, seq), 1)
    pos = rel + span * lax.broadcasted_iota(jnp.int32, (blocks, seq), 0)
    mz = ((rel >= span)[None] & (pos[None] < ends[:, :, None])).astype(jnp.float32)
    out = pl.pallas_call(
        conv_kernel,
        grid=(chans,),
        in_specs=[
            pl.BlockSpec((1, 1, width), lambda c: (c, 0, 0)),
            pl.BlockSpec((1, blocks, span), lambda c: (c, 0, 0)),
            pl.BlockSpec((blocks, span), lambda c: (0, 0)),
            pl.BlockSpec((2, blocks, seq), lambda c: (0, 0, 0)),
        ],
        out_specs=pl.BlockSpec((1, blocks, span), lambda c: (c, 0, 0)),
        out_shape=jax.ShapeDtypeStruct((chans, blocks, span), jnp.float32),
    )(f_ext, xb, docb, mz)
    return out.reshape(chans, seq)


def body(signal, gate, filt, bias, doc_ids, block_perm, out_weight):
    span = SPAN
    rows, chans = signal.shape
    blocks = block_perm.shape[0]
    seq = blocks * span
    n_ctx = seq // rows
    per_dev = chans // n_ctx
    ctx_index = lax.axis_index("ctx")

    inverse = jnp.zeros((blocks,), jnp.int32).at[block_perm].set(jnp.arange(blocks, dtype=jnp.int32))

    def slots_to_natural(a):
        return jnp.take(a.reshape(per_dev, blocks, span), inverse, axis=1).reshape(per_dev, seq)

    packed = jnp.stack(
        [a.reshape(rows, n_ctx, per_dev) for a in (signal, gate, filt)], axis=2
    ).reshape(rows, n_ctx * 3 * per_dev)
    arrived = lax.all_to_all(packed, "ctx", 1, 0, tiled=True).T
    x_cm = slots_to_natural(arrived[:per_dev])
    g_cm = slots_to_natural(arrived[per_dev : 2 * per_dev])
    f_cm = arrived[2 * per_dev :]
    bias_cm = lax.dynamic_slice_in_dim(bias, ctx_index * per_dev, per_dev)
    conv = pallas_conv(x_cm, f_cm, doc_ids)
    gated = (
        g_cm.astype(jnp.float32) * (conv + bias_cm[:, None] * x_cm.astype(jnp.float32))
    ).astype(jnp.bfloat16)
    gated_slots = jnp.take(gated.reshape(per_dev, blocks, span), block_perm, axis=1)
    gated_slots = gated_slots.reshape(per_dev, seq).T
    gated_local = lax.all_to_all(gated_slots, "ctx", 0, 1, tiled=True)
    tp_index = lax.axis_index("tp")
    n_tp = out_weight.shape[1] // chans
    high, core = tp_index // 2, tp_index % 2
    w_split = out_weight.reshape(chans, n_tp // 2, 2, chans)
    w_other = lax.dynamic_index_in_dim(w_split, 1 - core, axis=2, keepdims=False)
    p_other = jnp.dot(
        gated_local, w_other.reshape(chans, -1), preferred_element_type=jnp.float32
    )
    recv_core = lax.ppermute(p_other, "tp", [(i, i ^ 1) for i in range(n_tp)])
    w_mine = lax.dynamic_index_in_dim(w_split, core, axis=2, keepdims=False)
    p_mine = jnp.dot(gated_local, w_mine.reshape(chans, -1), preferred_element_type=jnp.float32)
    p_mine = p_mine + recv_core
    send_high = lax.dynamic_slice_in_dim(p_mine, (1 - high) * chans, chans, axis=1)
    keep_high = lax.dynamic_slice_in_dim(p_mine, high * chans, chans, axis=1)
    recv_high = lax.ppermute(send_high, "tp", [(i, i ^ 2) for i in range(n_tp)])
    return (keep_high + recv_high).astype(jnp.bfloat16)


def solution(mesh):
    return jax.shard_map(
        body,
        mesh=mesh,
        in_specs=(P("ctx", "tp"), P("ctx", "tp"), P("ctx", "tp"), P("tp"), P(), P(), P("tp", None)),
        out_specs=P("ctx", "tp"),
        check_vma=False,
    )
```

```python
import jax
import jax.numpy as jnp
from jax import lax
from jax.experimental import pallas as pl
from jax.experimental.pallas import tpu as pltpu
from jax.sharding import PartitionSpec as P

SPAN = 64
DOC_COUNT = 4


def conv_kernel(f_ref, x_ref, doc_ref, mz_ref, y_ref):
    blocks, span = x_ref.shape[1], x_ref.shape[2]
    seq = blocks * span
    width = f_ref.shape[2]
    lanes = 2 * span
    fb = jnp.broadcast_to(f_ref[0].astype(jnp.float32), (span, width))
    tt = pltpu.roll(fb, 0, 1, stride=1, stride_axis=0)[:, :seq].astype(jnp.bfloat16)
    x = x_ref[0]
    docs = doc_ref[...]
    lead = docs[:, 0:1]
    last = docs[:, span - 1 : span]
    zero = jnp.zeros_like(x)
    x_lead = jnp.where(docs == lead, x, zero)
    x_last = jnp.where((docs == last) & (docs != lead), x, zero)
    z_lead = jnp.dot(x_lead, tt, preferred_element_type=jnp.float32)
    z_last = jnp.dot(x_last, tt, preferred_element_type=jnp.float32)
    zm = z_lead * mz_ref[0] + z_last * mz_ref[1]
    acc = zm[:, :lanes]
    for pair in range(1, seq // lanes):
        acc = acc + pltpu.roll(zm[:, pair * lanes : (pair + 1) * lanes], 2 * pair, 0)
    y = acc[:, :span] + pltpu.roll(acc[:, span:], 1, 0)
    near = tt[:, :span]
    planes = jnp.concatenate([jnp.where(docs == doc, x, zero) for doc in range(DOC_COUNT)], axis=0)
    local = jnp.dot(planes, near, preferred_element_type=jnp.float32)
    for doc in range(DOC_COUNT):
        y = y + jnp.where(docs == doc, local[doc * blocks : (doc + 1) * blocks], 0.0)
    y_ref[0] = y


def pallas_conv(x_cm, f_cm, doc_ids):
    chans, seq = x_cm.shape
    span = SPAN
    blocks = seq // span
    width = seq + 2 * span
    f_ext = jnp.pad(f_cm, ((0, 0), (0, width - seq))).reshape(chans, 1, width)
    xb = x_cm.reshape(chans, blocks, span)
    docb = doc_ids.reshape(blocks, span)
    ends = jnp.sum(doc_ids[None, None, :] <= jnp.stack([docb[:, 0], docb[:, -1]])[:, :, None], axis=2)
    rel = lax.broadcasted_iota(jnp.int32, (blocks, seq), 1)
    pos = rel + span * lax.broadcasted_iota(jnp.int32, (blocks, seq), 0)
    mz = ((rel >= span)[None] & (pos[None] < ends[:, :, None])).astype(jnp.float32)
    out = pl.pallas_call(
        conv_kernel,
        grid=(chans,),
        in_specs=[
            pl.BlockSpec((1, 1, width), lambda c: (c, 0, 0)),
            pl.BlockSpec((1, blocks, span), lambda c: (c, 0, 0)),
            pl.BlockSpec((blocks, span), lambda c: (0, 0)),
            pl.BlockSpec((2, blocks, seq), lambda c: (0, 0, 0)),
        ],
        out_specs=pl.BlockSpec((1, blocks, span), lambda c: (c, 0, 0)),
        out_shape=jax.ShapeDtypeStruct((chans, blocks, span), jnp.float32),
    )(f_ext, xb, docb, mz)
    return out.reshape(chans, seq)


def body(signal, gate, filt, bias, doc_ids, block_perm, out_weight):
    span = SPAN
    rows, chans = signal.shape
    blocks = block_perm.shape[0]
    seq = blocks * span
    n_ctx = seq // rows
    per_dev = chans // n_ctx
    ctx_index = lax.axis_index("ctx")

    inverse = jnp.zeros((blocks,), jnp.int32).at[block_perm].set(jnp.arange(blocks, dtype=jnp.int32))

    def slots_to_natural(a):
        return jnp.take(a.reshape(per_dev, blocks, span), inverse, axis=1).reshape(per_dev, seq)

    packed = jnp.stack(
        [a.reshape(rows, n_ctx, per_dev) for a in (signal, filt)], axis=2
    ).reshape(rows, n_ctx * 2 * per_dev)
    arrived = lax.all_to_all(packed, "ctx", 1, 0, tiled=True).T
    x_cm = slots_to_natural(arrived[:per_dev])
    f_cm = arrived[per_dev:]
    bias_cm = lax.dynamic_slice_in_dim(bias, ctx_index * per_dev, per_dev)
    conv = pallas_conv(x_cm, f_cm, doc_ids)
    pre = (conv + bias_cm[:, None] * x_cm.astype(jnp.float32)).astype(jnp.bfloat16)
    pre_slots = jnp.take(pre.reshape(per_dev, blocks, span), block_perm, axis=1)
    pre_slots = pre_slots.reshape(per_dev, seq).T
    pre_local = lax.all_to_all(pre_slots, "ctx", 0, 1, tiled=True)
    gated_local = (gate.astype(jnp.float32) * pre_local.astype(jnp.float32)).astype(jnp.bfloat16)
    tp_index = lax.axis_index("tp")
    n_tp = out_weight.shape[1] // chans
    high, core = tp_index // 2, tp_index % 2
    w_split = out_weight.reshape(chans, n_tp // 2, 2, chans)
    w_other = lax.dynamic_index_in_dim(w_split, 1 - core, axis=2, keepdims=False)
    p_other = jnp.dot(
        gated_local, w_other.reshape(chans, -1), preferred_element_type=jnp.float32
    )
    recv_core = lax.ppermute(p_other.astype(jnp.bfloat16), "tp", [(i, i ^ 1) for i in range(n_tp)])
    w_mine = lax.dynamic_index_in_dim(w_split, core, axis=2, keepdims=False)
    p_mine = jnp.dot(gated_local, w_mine.reshape(chans, -1), preferred_element_type=jnp.float32)
    p_mine = p_mine + recv_core.astype(jnp.float32)
    send_high = lax.dynamic_slice_in_dim(p_mine, (1 - high) * chans, chans, axis=1)
    keep_high = lax.dynamic_slice_in_dim(p_mine, high * chans, chans, axis=1)
    recv_high = lax.ppermute(
        send_high.astype(jnp.bfloat16), "tp", [(i, i ^ 2) for i in range(n_tp)]
    )
    return (keep_high + recv_high.astype(jnp.float32)).astype(jnp.bfloat16)


def solution(mesh):
    return jax.shard_map(
        body,
        mesh=mesh,
        in_specs=(P("ctx", "tp"), P("ctx", "tp"), P("ctx", "tp"), P("tp"), P(), P(), P("tp", None)),
        out_specs=P("ctx", "tp"),
        check_vma=False,
    )
```

```python
import jax
import jax.numpy as jnp
from jax import lax
from jax.experimental import pallas as pl
from jax.experimental.pallas import tpu as pltpu
from jax.sharding import PartitionSpec as P

SPAN = 64
DOC_COUNT = 4


CHANNELS_PER_STEP = 2


def conv_kernel(bias_ref, f_ref, x_ref, doc_ref, mz_ref, y_ref):
    blocks, span = x_ref.shape[1], x_ref.shape[2]
    seq = blocks * span
    lanes = 2 * span
    docs = doc_ref[...]
    lead = docs[:, 0:1]
    last = docs[:, span - 1 : span]
    lead_rows = docs == lead
    last_rows = (docs == last) & (docs != lead)
    doc_rows = [docs == doc for doc in range(DOC_COUNT)]
    for k in range(x_ref.shape[0]):
        channel = pl.program_id(0) * x_ref.shape[0] + k
        frow = f_ref[k].astype(jnp.float32)
        frow = jnp.concatenate([frow, jnp.zeros((1, lanes), jnp.float32)], axis=1)
        fb = jnp.broadcast_to(frow, (span, seq + lanes))
        tt = pltpu.roll(fb, 0, 1, stride=1, stride_axis=0)[:, :seq].astype(jnp.bfloat16)
        x = x_ref[k]
        zero = jnp.zeros_like(x)
        z_lead = jnp.dot(jnp.where(lead_rows, x, zero), tt, preferred_element_type=jnp.float32)
        z_last = jnp.dot(jnp.where(last_rows, x, zero), tt, preferred_element_type=jnp.float32)
        zm = z_lead * mz_ref[0] + z_last * mz_ref[1]
        acc = zm[:, :lanes]
        for pair in range(1, seq // lanes):
            acc = acc + pltpu.roll(zm[:, pair * lanes : (pair + 1) * lanes], 2 * pair, 0)
        y = acc[:, :span] + pltpu.roll(acc[:, span:], 1, 0)
        planes = jnp.concatenate([jnp.where(rows, x, zero) for rows in doc_rows], axis=0)
        local = jnp.dot(planes, tt[:, :span], preferred_element_type=jnp.float32)
        for doc in range(DOC_COUNT):
            y = y + jnp.where(doc_rows[doc], local[doc * blocks : (doc + 1) * blocks], 0.0)
        y = y + bias_ref[channel] * x.astype(jnp.float32)
        y_ref[k] = y.astype(y_ref.dtype)


def pallas_conv(x_cm, f_cm, doc_ids, bias_cm):
    chans, seq = x_cm.shape
    span = SPAN
    blocks = seq // span
    step = CHANNELS_PER_STEP
    xb = x_cm.reshape(chans, blocks, span)
    docb = doc_ids.reshape(blocks, span)
    ends = jnp.sum(doc_ids[None, None, :] <= jnp.stack([docb[:, 0], docb[:, -1]])[:, :, None], axis=2)
    rel = lax.broadcasted_iota(jnp.int32, (blocks, seq), 1)
    pos = rel + span * lax.broadcasted_iota(jnp.int32, (blocks, seq), 0)
    mz = ((rel >= span)[None] & (pos[None] < ends[:, :, None])).astype(jnp.float32)
    return pl.pallas_call(
        conv_kernel,
        grid=(chans // step,),
        in_specs=[
            pl.BlockSpec(memory_space=pltpu.SMEM),
            pl.BlockSpec((step, 1, seq), lambda c: (c, 0, 0)),
            pl.BlockSpec((step, blocks, span), lambda c: (c, 0, 0)),
            pl.BlockSpec((blocks, span), lambda c: (0, 0)),
            pl.BlockSpec((2, blocks, seq), lambda c: (0, 0, 0)),
        ],
        out_specs=pl.BlockSpec((step, blocks, span), lambda c: (c, 0, 0)),
        out_shape=jax.ShapeDtypeStruct((chans, blocks, span), jnp.bfloat16),
    )(bias_cm, f_cm.reshape(chans, 1, seq), xb, docb, mz)


def body(signal, gate, filt, bias, doc_ids, block_perm, out_weight):
    span = SPAN
    rows, chans = signal.shape
    blocks = block_perm.shape[0]
    seq = blocks * span
    n_ctx = seq // rows
    per_dev = chans // n_ctx
    ctx_index = lax.axis_index("ctx")

    inverse = jnp.zeros((blocks,), jnp.int32).at[block_perm].set(jnp.arange(blocks, dtype=jnp.int32))

    def slots_to_natural(a):
        return jnp.take(a.reshape(per_dev, blocks, span), inverse, axis=1).reshape(per_dev, seq)

    packed = jnp.stack(
        [a.reshape(rows, n_ctx, per_dev) for a in (signal, filt)], axis=2
    ).reshape(rows, n_ctx * 2 * per_dev)
    arrived = lax.all_to_all(packed, "ctx", 1, 0, tiled=True).T
    x_cm = slots_to_natural(arrived[:per_dev])
    f_cm = arrived[per_dev:]
    bias_cm = lax.dynamic_slice_in_dim(bias, ctx_index * per_dev, per_dev)
    pre = pallas_conv(x_cm, f_cm, doc_ids, bias_cm)
    pre_slots = jnp.take(pre, block_perm, axis=1)
    pre_slots = pre_slots.reshape(per_dev, seq).T
    pre_local = lax.all_to_all(pre_slots, "ctx", 0, 1, tiled=True)
    gated_local = (gate.astype(jnp.float32) * pre_local.astype(jnp.float32)).astype(jnp.bfloat16)
    tp_index = lax.axis_index("tp")
    n_tp = out_weight.shape[1] // chans
    high, core = tp_index // 2, tp_index % 2
    w_split = out_weight.reshape(chans, n_tp // 2, 2, chans)
    w_other = lax.dynamic_index_in_dim(w_split, 1 - core, axis=2, keepdims=False)
    p_other = jnp.dot(
        gated_local, w_other.reshape(chans, -1), preferred_element_type=jnp.float32
    )
    recv_core = lax.ppermute(p_other.astype(jnp.bfloat16), "tp", [(i, i ^ 1) for i in range(n_tp)])
    w_mine = lax.dynamic_index_in_dim(w_split, core, axis=2, keepdims=False)
    p_mine = jnp.dot(gated_local, w_mine.reshape(chans, -1), preferred_element_type=jnp.float32)
    p_mine = p_mine + recv_core.astype(jnp.float32)
    send_high = lax.dynamic_slice_in_dim(p_mine, (1 - high) * chans, chans, axis=1)
    keep_high = lax.dynamic_slice_in_dim(p_mine, high * chans, chans, axis=1)
    recv_high = lax.ppermute(
        send_high.astype(jnp.bfloat16), "tp", [(i, i ^ 2) for i in range(n_tp)]
    )
    return (keep_high + recv_high.astype(jnp.float32)).astype(jnp.bfloat16)


def solution(mesh):
    return jax.shard_map(
        body,
        mesh=mesh,
        in_specs=(P("ctx", "tp"), P("ctx", "tp"), P("ctx", "tp"), P("tp"), P(), P(), P("tp", None)),
        out_specs=P("ctx", "tp"),
        check_vma=False,
    )
```

```python
import jax
import jax.numpy as jnp
from jax import lax
from jax.experimental import pallas as pl
from jax.experimental.pallas import tpu as pltpu
from jax.sharding import PartitionSpec as P

SPAN = 64
DOC_COUNT = 4


CHANNELS_PER_STEP = 4


def conv_kernel(bias_ref, f_ref, x_ref, doc_ref, mz_ref, y_ref):
    blocks, span = x_ref.shape[1], x_ref.shape[2]
    seq = blocks * span
    lanes = 2 * span
    docs = doc_ref[...]
    lead = docs[:, 0:1]
    last = docs[:, span - 1 : span]
    lead_rows = docs == lead
    last_rows = (docs == last) & (docs != lead)
    doc_rows = [docs == doc for doc in range(DOC_COUNT)]
    for k in range(x_ref.shape[0]):
        channel = pl.program_id(0) * x_ref.shape[0] + k
        frow = f_ref[k].astype(jnp.float32)
        frow = jnp.concatenate([frow, jnp.zeros((1, lanes), jnp.float32)], axis=1)
        fb = jnp.broadcast_to(frow, (span, seq + lanes))
        tt = pltpu.roll(fb, 0, 1, stride=1, stride_axis=0)[:, :seq].astype(jnp.bfloat16)
        x = x_ref[k]
        zero = jnp.zeros_like(x)
        z_lead = jnp.dot(jnp.where(lead_rows, x, zero), tt, preferred_element_type=jnp.float32)
        z_last = jnp.dot(jnp.where(last_rows, x, zero), tt, preferred_element_type=jnp.float32)
        zm = z_lead * mz_ref[0] + z_last * mz_ref[1]
        acc = zm[:, :lanes]
        for pair in range(1, seq // lanes):
            acc = acc + pltpu.roll(zm[:, pair * lanes : (pair + 1) * lanes], 2 * pair, 0)
        y = acc[:, :span] + pltpu.roll(acc[:, span:], 1, 0)
        planes = jnp.concatenate([jnp.where(rows, x, zero) for rows in doc_rows], axis=0)
        local = jnp.dot(planes, tt[:, :span], preferred_element_type=jnp.float32)
        for doc in range(DOC_COUNT):
            y = y + jnp.where(doc_rows[doc], local[doc * blocks : (doc + 1) * blocks], 0.0)
        y = y + bias_ref[channel] * x.astype(jnp.float32)
        y_ref[k] = y.astype(y_ref.dtype)


def pallas_conv(x_cm, f_cm, doc_ids, bias_cm):
    chans, seq = x_cm.shape
    span = SPAN
    blocks = seq // span
    step = CHANNELS_PER_STEP
    xb = x_cm.reshape(chans, blocks, span)
    docb = doc_ids.reshape(blocks, span)
    ends = jnp.sum(doc_ids[None, None, :] <= jnp.stack([docb[:, 0], docb[:, -1]])[:, :, None], axis=2)
    rel = lax.broadcasted_iota(jnp.int32, (blocks, seq), 1)
    pos = rel + span * lax.broadcasted_iota(jnp.int32, (blocks, seq), 0)
    mz = ((rel >= span)[None] & (pos[None] < ends[:, :, None])).astype(jnp.float32)
    return pl.pallas_call(
        conv_kernel,
        grid=(chans // step,),
        in_specs=[
            pl.BlockSpec(memory_space=pltpu.SMEM),
            pl.BlockSpec((step, 1, seq), lambda c: (c, 0, 0)),
            pl.BlockSpec((step, blocks, span), lambda c: (c, 0, 0)),
            pl.BlockSpec((blocks, span), lambda c: (0, 0)),
            pl.BlockSpec((2, blocks, seq), lambda c: (0, 0, 0)),
        ],
        out_specs=pl.BlockSpec((step, blocks, span), lambda c: (c, 0, 0)),
        out_shape=jax.ShapeDtypeStruct((chans, blocks, span), jnp.bfloat16),
    )(bias_cm, f_cm.reshape(chans, 1, seq), xb, docb, mz)


def body(signal, gate, filt, bias, doc_ids, block_perm, out_weight):
    span = SPAN
    rows, chans = signal.shape
    blocks = block_perm.shape[0]
    seq = blocks * span
    n_ctx = seq // rows
    per_dev = chans // n_ctx
    ctx_index = lax.axis_index("ctx")

    inverse = jnp.zeros((blocks,), jnp.int32).at[block_perm].set(jnp.arange(blocks, dtype=jnp.int32))

    def slots_to_natural(a):
        return jnp.take(a.reshape(per_dev, blocks, span), inverse, axis=1).reshape(per_dev, seq)

    packed = jnp.stack(
        [a.reshape(rows, n_ctx, per_dev) for a in (signal, filt)], axis=2
    ).reshape(rows, n_ctx * 2 * per_dev)
    arrived = lax.all_to_all(packed, "ctx", 1, 0, tiled=True).T
    x_cm = slots_to_natural(arrived[:per_dev])
    f_cm = arrived[per_dev:]
    bias_cm = lax.dynamic_slice_in_dim(bias, ctx_index * per_dev, per_dev)
    pre = pallas_conv(x_cm, f_cm, doc_ids, bias_cm)
    pre_slots = jnp.take(pre, block_perm, axis=1)
    pre_slots = pre_slots.reshape(per_dev, seq).T
    pre_local = lax.all_to_all(pre_slots, "ctx", 0, 1, tiled=True)
    gated_local = (gate.astype(jnp.float32) * pre_local.astype(jnp.float32)).astype(jnp.bfloat16)
    tp_index = lax.axis_index("tp")
    n_tp = out_weight.shape[1] // chans
    total = None
    for offset in range(n_tp):
        target = (tp_index + offset) % n_tp
        w_cols = lax.dynamic_slice_in_dim(out_weight, target * chans, chans, axis=1)
        part = jnp.dot(gated_local, w_cols, preferred_element_type=jnp.float32)
        if offset:
            pairs = [(i, (i + offset) % n_tp) for i in range(n_tp)]
            part = lax.ppermute(part.astype(jnp.bfloat16), "tp", pairs).astype(jnp.float32)
        total = part if total is None else total + part
    return total.astype(jnp.bfloat16)


def solution(mesh):
    return jax.shard_map(
        body,
        mesh=mesh,
        in_specs=(P("ctx", "tp"), P("ctx", "tp"), P("ctx", "tp"), P("tp"), P(), P(), P("tp", None)),
        out_specs=P("ctx", "tp"),
        check_vma=False,
    )
```

```python
import jax
import jax.numpy as jnp
from jax import lax
from jax.experimental import pallas as pl
from jax.experimental.pallas import tpu as pltpu
from jax.sharding import PartitionSpec as P

SPAN = 64
DOC_COUNT = 4


CHANNELS_PER_STEP = 4


def conv_kernel(bias_ref, f_ref, x_ref, doc_ref, mask_ref, y_ref):
    blocks, span = x_ref.shape[1], x_ref.shape[2]
    seq = blocks * span
    lanes = 2 * span
    docs = doc_ref[...]
    lead = docs[:, span - 1 : span]
    lead_rows = docs == lead
    doc_rows = [docs == doc for doc in range(DOC_COUNT)]
    contract = (((1,), (1,)), ((), ()))
    for k in range(x_ref.shape[0]):
        channel = pl.program_id(0) * x_ref.shape[0] + k
        frow = f_ref[k].astype(jnp.float32)
        frow = jnp.concatenate([frow, jnp.zeros((1, lanes), jnp.float32)], axis=1)
        fb = jnp.broadcast_to(frow, (span, seq + lanes))
        tt = pltpu.roll(fb, 0, 1, stride=1, stride_axis=0)[:, :seq].astype(jnp.bfloat16)
        x = x_ref[k]
        xf = x.astype(jnp.float32)
        pair = jnp.concatenate([xf, pltpu.roll(xf, 1, 0)], axis=1)
        src = jnp.concatenate(
            [pair] + [pltpu.roll(pair, 2 * p, 0) for p in range(1, seq // lanes)], axis=1
        )
        src = (src * mask_ref[...]).astype(jnp.bfloat16)
        y = lax.dot_general(src, tt, contract, preferred_element_type=jnp.float32)
        y = jnp.where(lead_rows, y, 0.0)
        zero = jnp.zeros_like(x)
        planes = jnp.concatenate([jnp.where(rows, x, zero) for rows in doc_rows], axis=0)
        local = lax.dot_general(planes, tt[:, :span], contract, preferred_element_type=jnp.float32)
        for doc in range(DOC_COUNT):
            rows = doc_rows[doc] & (lead != doc)
            y = y + jnp.where(rows, local[doc * blocks : (doc + 1) * blocks], 0.0)
        y = y + bias_ref[channel] * xf
        y_ref[k] = y.astype(y_ref.dtype)


def pallas_conv(x_cm, f_cm, doc_ids, bias_cm):
    chans, seq = x_cm.shape
    span = SPAN
    blocks = seq // span
    step = CHANNELS_PER_STEP
    xb = x_cm.reshape(chans, blocks, span)[:, :, ::-1]
    docb = doc_ids.reshape(blocks, span)
    starts = jnp.sum(doc_ids[None, :] < docb[:, :1], axis=1)
    lag = lax.broadcasted_iota(jnp.int32, (blocks, blocks, span), 1)
    tgt = lax.broadcasted_iota(jnp.int32, (blocks, blocks, span), 0)
    off = span - 1 - lax.broadcasted_iota(jnp.int32, (blocks, blocks, span), 2)
    mask = (tgt >= lag) & (span * (tgt - lag) + off >= starts[:, None, None])
    mask = mask.astype(jnp.float32).reshape(blocks, seq)
    out = pl.pallas_call(
        conv_kernel,
        grid=(chans // step,),
        in_specs=[
            pl.BlockSpec(memory_space=pltpu.SMEM),
            pl.BlockSpec((step, 1, seq), lambda c: (c, 0, 0)),
            pl.BlockSpec((step, blocks, span), lambda c: (c, 0, 0)),
            pl.BlockSpec((blocks, span), lambda c: (0, 0)),
            pl.BlockSpec((blocks, seq), lambda c: (0, 0)),
        ],
        out_specs=pl.BlockSpec((step, blocks, span), lambda c: (c, 0, 0)),
        out_shape=jax.ShapeDtypeStruct((chans, blocks, span), jnp.bfloat16),
    )(bias_cm, f_cm.reshape(chans, 1, seq), xb, docb[:, ::-1], mask)
    return out[:, :, ::-1]


def body(signal, gate, filt, bias, doc_ids, block_perm, out_weight):
    span = SPAN
    rows, chans = signal.shape
    blocks = block_perm.shape[0]
    seq = blocks * span
    n_ctx = seq // rows
    per_dev = chans // n_ctx
    ctx_index = lax.axis_index("ctx")

    inverse = jnp.zeros((blocks,), jnp.int32).at[block_perm].set(jnp.arange(blocks, dtype=jnp.int32))

    def slots_to_natural(a):
        return jnp.take(a.reshape(per_dev, blocks, span), inverse, axis=1).reshape(per_dev, seq)

    packed = jnp.stack(
        [a.reshape(rows, n_ctx, per_dev) for a in (signal, filt)], axis=2
    ).reshape(rows, n_ctx * 2 * per_dev)
    arrived = lax.all_to_all(packed, "ctx", 1, 0, tiled=True).T
    x_cm = slots_to_natural(arrived[:per_dev])
    f_cm = arrived[per_dev:]
    bias_cm = lax.dynamic_slice_in_dim(bias, ctx_index * per_dev, per_dev)
    pre = pallas_conv(x_cm, f_cm, doc_ids, bias_cm)
    pre_slots = jnp.take(pre, block_perm, axis=1)
    pre_slots = pre_slots.reshape(per_dev, seq).T
    pre_local = lax.all_to_all(pre_slots, "ctx", 0, 1, tiled=True)
    gated_local = (gate.astype(jnp.float32) * pre_local.astype(jnp.float32)).astype(jnp.bfloat16)
    tp_index = lax.axis_index("tp")
    n_tp = out_weight.shape[1] // chans
    total = None
    for offset in range(n_tp):
        target = (tp_index + offset) % n_tp
        w_cols = lax.dynamic_slice_in_dim(out_weight, target * chans, chans, axis=1)
        part = jnp.dot(gated_local, w_cols, preferred_element_type=jnp.float32)
        if offset:
            pairs = [(i, (i + offset) % n_tp) for i in range(n_tp)]
            part = lax.ppermute(part.astype(jnp.bfloat16), "tp", pairs).astype(jnp.float32)
        total = part if total is None else total + part
    return total.astype(jnp.bfloat16)


def solution(mesh):
    return jax.shard_map(
        body,
        mesh=mesh,
        in_specs=(P("ctx", "tp"), P("ctx", "tp"), P("ctx", "tp"), P("tp"), P(), P(), P("tp", None)),
        out_specs=P("ctx", "tp"),
        check_vma=False,
    )
```

```python
import jax
import jax.numpy as jnp
from jax import lax
from jax.experimental import pallas as pl
from jax.experimental.pallas import tpu as pltpu
from jax.sharding import PartitionSpec as P

SPAN = 64
DOC_COUNT = 4


CHANNELS_PER_STEP = 4


def exact_dot(a, b):
    return jnp.dot(a, b, preferred_element_type=jnp.float32).astype(a.dtype)


def conv_kernel(bias_ref, f_ref, x_ref, doc_ref, mask_ref, perm_ref, y_ref):
    blocks, span = x_ref.shape[1], x_ref.shape[2]
    seq = blocks * span
    lanes = 2 * span
    docs = doc_ref[...]
    lead = docs[:, span - 1 : span]
    lead_rows = docs == lead
    doc_rows = [docs == doc for doc in range(DOC_COUNT)]
    contract = (((1,), (1,)), ((), ()))
    for k in range(x_ref.shape[0]):
        channel = pl.program_id(0) * x_ref.shape[0] + k
        frow = f_ref[k].astype(jnp.float32)
        frow = jnp.concatenate([frow, jnp.zeros((1, lanes), jnp.float32)], axis=1)
        fb = jnp.broadcast_to(frow, (span, seq + lanes))
        tt = pltpu.roll(fb, 0, 1, stride=1, stride_axis=0)[:, :seq].astype(jnp.bfloat16)
        x = exact_dot(perm_ref[0], exact_dot(x_ref[k], perm_ref[2]))
        xf = x.astype(jnp.float32)
        pair = jnp.concatenate([xf, pltpu.roll(xf, 1, 0)], axis=1)
        src = jnp.concatenate(
            [pair] + [pltpu.roll(pair, 2 * p, 0) for p in range(1, seq // lanes)], axis=1
        )
        src = (src * mask_ref[...]).astype(jnp.bfloat16)
        y = lax.dot_general(src, tt, contract, preferred_element_type=jnp.float32)
        y = jnp.where(lead_rows, y, 0.0)
        zero = jnp.zeros_like(x)
        planes = jnp.concatenate([jnp.where(rows, x, zero) for rows in doc_rows], axis=0)
        local = lax.dot_general(planes, tt[:, :span], contract, preferred_element_type=jnp.float32)
        for doc in range(DOC_COUNT):
            rows = doc_rows[doc] & (lead != doc)
            y = y + jnp.where(rows, local[doc * blocks : (doc + 1) * blocks], 0.0)
        y = y + bias_ref[channel] * xf
        y = y.astype(y_ref.dtype)
        y_ref[k] = exact_dot(perm_ref[1], exact_dot(y, perm_ref[2]))


def pallas_conv(x_slots, f_cm, doc_ids, bias_cm, block_perm):
    chans, seq = x_slots.shape
    span = SPAN
    blocks = seq // span
    step = CHANNELS_PER_STEP
    xb = x_slots.reshape(chans, blocks, span)
    to_seq = (block_perm[None, :] == jnp.arange(blocks, dtype=jnp.int32)[:, None]).astype(x_slots.dtype)
    flip = jnp.eye(span, dtype=x_slots.dtype)[::-1]
    perms = jnp.stack([to_seq, to_seq.T, flip])
    docb = doc_ids.reshape(blocks, span)
    starts = jnp.sum(doc_ids[None, :] < docb[:, :1], axis=1)
    lag = lax.broadcasted_iota(jnp.int32, (blocks, blocks, span), 1)
    tgt = lax.broadcasted_iota(jnp.int32, (blocks, blocks, span), 0)
    off = span - 1 - lax.broadcasted_iota(jnp.int32, (blocks, blocks, span), 2)
    mask = (tgt >= lag) & (span * (tgt - lag) + off >= starts[:, None, None])
    mask = mask.astype(jnp.float32).reshape(blocks, seq)
    out = pl.pallas_call(
        conv_kernel,
        grid=(chans // step,),
        in_specs=[
            pl.BlockSpec(memory_space=pltpu.SMEM),
            pl.BlockSpec((step, 1, seq), lambda c: (c, 0, 0)),
            pl.BlockSpec((step, blocks, span), lambda c: (c, 0, 0)),
            pl.BlockSpec((blocks, span), lambda c: (0, 0)),
            pl.BlockSpec((blocks, seq), lambda c: (0, 0)),
            pl.BlockSpec((3, blocks, span), lambda c: (0, 0, 0)),
        ],
        out_specs=pl.BlockSpec((step, blocks, span), lambda c: (c, 0, 0)),
        out_shape=jax.ShapeDtypeStruct((chans, blocks, span), jnp.bfloat16),
    )(bias_cm, f_cm.reshape(chans, 1, seq), xb, docb[:, ::-1], mask, perms)
    return out


def body(signal, gate, filt, bias, doc_ids, block_perm, out_weight):
    span = SPAN
    rows, chans = signal.shape
    blocks = block_perm.shape[0]
    seq = blocks * span
    n_ctx = seq // rows
    per_dev = chans // n_ctx
    ctx_index = lax.axis_index("ctx")

    packed = jnp.stack(
        [a.reshape(rows, n_ctx, per_dev) for a in (signal, filt)], axis=2
    ).reshape(rows, n_ctx * 2 * per_dev)
    arrived = lax.all_to_all(packed, "ctx", 1, 0, tiled=True).T
    x_slots = arrived[:per_dev]
    f_cm = arrived[per_dev:]
    bias_cm = lax.dynamic_slice_in_dim(bias, ctx_index * per_dev, per_dev)
    pre_slots = pallas_conv(x_slots, f_cm, doc_ids, bias_cm, block_perm)
    pre_slots = pre_slots.reshape(per_dev, seq).T
    pre_local = lax.all_to_all(pre_slots, "ctx", 0, 1, tiled=True)
    gated_local = (gate.astype(jnp.float32) * pre_local.astype(jnp.float32)).astype(jnp.bfloat16)
    tp_index = lax.axis_index("tp")
    n_tp = out_weight.shape[1] // chans
    total = None
    for offset in range(n_tp):
        target = (tp_index + offset) % n_tp
        w_cols = lax.dynamic_slice_in_dim(out_weight, target * chans, chans, axis=1)
        part = jnp.dot(gated_local, w_cols, preferred_element_type=jnp.float32)
        if offset:
            pairs = [(i, (i + offset) % n_tp) for i in range(n_tp)]
            part = lax.ppermute(part.astype(jnp.bfloat16), "tp", pairs).astype(jnp.float32)
        total = part if total is None else total + part
    return total.astype(jnp.bfloat16)


def solution(mesh):
    return jax.shard_map(
        body,
        mesh=mesh,
        in_specs=(P("ctx", "tp"), P("ctx", "tp"), P("ctx", "tp"), P("tp"), P(), P(), P("tp", None)),
        out_specs=P("ctx", "tp"),
        check_vma=False,
    )
```

```python
import jax
import jax.numpy as jnp
from jax import lax
from jax.experimental import pallas as pl
from jax.experimental.pallas import tpu as pltpu
from jax.sharding import PartitionSpec as P

SPAN = 64
DOC_COUNT = 4


CHANNELS_PER_STEP = 4


def conv_kernel(bias_ref, f_ref, x_ref, doc_ref, mask_ref, y_ref):
    blocks, span = x_ref.shape[1], x_ref.shape[2]
    seq = blocks * span
    lanes = 2 * span
    width = seq + lanes
    docs = doc_ref[...]
    lead = docs[:, 0:1]
    lead_rows = docs == lead
    doc_rows = [docs == doc for doc in range(DOC_COUNT)]
    contract = (((1,), (1,)), ((), ()))
    for k in range(x_ref.shape[0]):
        channel = pl.program_id(0) * x_ref.shape[0] + k
        frow = f_ref[k].astype(jnp.float32)
        frow = jnp.concatenate([frow, jnp.zeros((1, lanes), jnp.float32)], axis=1)
        fb = jnp.broadcast_to(frow, (span, width))
        tt = pltpu.roll(fb, width - (span - 1), 1, stride=1, stride_axis=0)[:, :seq]
        tt = tt.astype(jnp.bfloat16)
        x = x_ref[k]
        xf = x.astype(jnp.float32)
        pair = jnp.concatenate([pltpu.roll(xf, 1, 0), xf], axis=1)
        src = jnp.concatenate(
            [pltpu.roll(pair, (blocks - 2 - 2 * p) % blocks, 0) for p in range(seq // lanes)], axis=1
        )
        src = (src * mask_ref[...]).astype(jnp.bfloat16)
        y = lax.dot_general(src, tt, contract, preferred_element_type=jnp.float32)
        y = jnp.where(lead_rows, y, 0.0)
        zero = jnp.zeros_like(x)
        planes = jnp.concatenate([jnp.where(rows, x, zero) for rows in doc_rows], axis=0)
        local = lax.dot_general(
            planes, tt[:, seq - span :], contract, preferred_element_type=jnp.float32
        )
        for doc in range(DOC_COUNT):
            rows = doc_rows[doc] & (lead != doc)
            y = y + jnp.where(rows, local[doc * blocks : (doc + 1) * blocks], 0.0)
        y = y + bias_ref[channel] * xf
        y_ref[k] = y.astype(y_ref.dtype)


def pallas_conv(x_cm, f_cm, doc_ids, bias_cm):
    chans, seq = x_cm.shape
    span = SPAN
    blocks = seq // span
    step = CHANNELS_PER_STEP
    xb = x_cm.reshape(chans, blocks, span)
    docb = doc_ids.reshape(blocks, span)
    starts = jnp.sum(doc_ids[None, :] < docb[:, :1], axis=1)
    tgt = lax.broadcasted_iota(jnp.int32, (blocks, blocks, span), 0)
    src_block = tgt - (blocks - 1) + lax.broadcasted_iota(jnp.int32, (blocks, blocks, span), 1)
    off = lax.broadcasted_iota(jnp.int32, (blocks, blocks, span), 2)
    mask = (src_block >= 0) & (span * src_block + off >= starts[:, None, None])
    mask = mask.astype(jnp.float32).reshape(blocks, seq)
    return pl.pallas_call(
        conv_kernel,
        grid=(chans // step,),
        in_specs=[
            pl.BlockSpec(memory_space=pltpu.SMEM),
            pl.BlockSpec((step, 1, seq), lambda c: (c, 0, 0)),
            pl.BlockSpec((step, blocks, span), lambda c: (c, 0, 0)),
            pl.BlockSpec((blocks, span), lambda c: (0, 0)),
            pl.BlockSpec((blocks, seq), lambda c: (0, 0)),
        ],
        out_specs=pl.BlockSpec((step, blocks, span), lambda c: (c, 0, 0)),
        out_shape=jax.ShapeDtypeStruct((chans, blocks, span), jnp.bfloat16),
    )(bias_cm, f_cm[:, ::-1].reshape(chans, 1, seq), xb, docb, mask)


def body(signal, gate, filt, bias, doc_ids, block_perm, out_weight):
    span = SPAN
    rows, chans = signal.shape
    blocks = block_perm.shape[0]
    seq = blocks * span
    n_ctx = seq // rows
    per_dev = chans // n_ctx
    ctx_index = lax.axis_index("ctx")

    inverse = jnp.zeros((blocks,), jnp.int32).at[block_perm].set(jnp.arange(blocks, dtype=jnp.int32))

    def slots_to_natural(a):
        return jnp.take(a.reshape(per_dev, blocks, span), inverse, axis=1).reshape(per_dev, seq)

    packed = jnp.stack(
        [a.reshape(rows, n_ctx, per_dev) for a in (signal, filt)], axis=2
    ).reshape(rows, n_ctx * 2 * per_dev)
    arrived = lax.all_to_all(packed, "ctx", 1, 0, tiled=True).T
    x_cm = slots_to_natural(arrived[:per_dev])
    f_cm = arrived[per_dev:]
    bias_cm = lax.dynamic_slice_in_dim(bias, ctx_index * per_dev, per_dev)
    pre = pallas_conv(x_cm, f_cm, doc_ids, bias_cm)
    pre_slots = jnp.take(pre, block_perm, axis=1)
    pre_slots = pre_slots.reshape(per_dev, seq).T
    pre_local = lax.all_to_all(pre_slots, "ctx", 0, 1, tiled=True)
    gated_local = (gate.astype(jnp.float32) * pre_local.astype(jnp.float32)).astype(jnp.bfloat16)
    tp_index = lax.axis_index("tp")
    n_tp = out_weight.shape[1] // chans
    total = None
    for offset in range(n_tp):
        target = (tp_index + offset) % n_tp
        w_cols = lax.dynamic_slice_in_dim(out_weight, target * chans, chans, axis=1)
        part = jnp.dot(gated_local, w_cols, preferred_element_type=jnp.float32)
        if offset:
            pairs = [(i, (i + offset) % n_tp) for i in range(n_tp)]
            part = lax.ppermute(part.astype(jnp.bfloat16), "tp", pairs).astype(jnp.float32)
        total = part if total is None else total + part
    return total.astype(jnp.bfloat16)


def solution(mesh):
    return jax.shard_map(
        body,
        mesh=mesh,
        in_specs=(P("ctx", "tp"), P("ctx", "tp"), P("ctx", "tp"), P("tp"), P(), P(), P("tp", None)),
        out_specs=P("ctx", "tp"),
        check_vma=False,
    )
```

```python
import jax
import jax.numpy as jnp
from jax import lax
from jax.experimental import pallas as pl
from jax.experimental.pallas import tpu as pltpu
from jax.sharding import PartitionSpec as P

SPAN = 64
DOC_COUNT = 4


CHANNELS_PER_STEP = 4


def conv_kernel(bias_ref, f_ref, x_ref, doc_ref, mask_ref, y_ref):
    blocks, span = x_ref.shape[1], x_ref.shape[2]
    seq = blocks * span
    lanes = 2 * span
    docs = doc_ref[...]
    lead = docs[:, span - 1 : span]
    lead_rows = docs == lead
    doc_rows = [docs == doc for doc in range(DOC_COUNT)]
    contract = (((1,), (1,)), ((), ()))
    for k in range(x_ref.shape[0]):
        channel = pl.program_id(0) * x_ref.shape[0] + k
        frow = f_ref[k].astype(jnp.float32)
        frow = jnp.concatenate([frow, jnp.zeros((1, lanes), jnp.float32)], axis=1)
        fb = jnp.broadcast_to(frow, (span, seq + lanes))
        tt = pltpu.roll(fb, 0, 1, stride=1, stride_axis=0)[:, :seq].astype(jnp.bfloat16)
        x = x_ref[k]
        xf = x.astype(jnp.float32)
        pair = jnp.concatenate([xf, pltpu.roll(xf, 1, 0)], axis=1)
        src = jnp.concatenate(
            [pair] + [pltpu.roll(pair, 2 * p, 0) for p in range(1, seq // lanes)], axis=1
        )
        src = (src * mask_ref[...]).astype(jnp.bfloat16)
        y = lax.dot_general(src, tt, contract, preferred_element_type=jnp.float32)
        y = jnp.where(lead_rows, y, 0.0)
        zero = jnp.zeros_like(x)
        planes = jnp.concatenate([jnp.where(rows, x, zero) for rows in doc_rows], axis=0)
        local = lax.dot_general(planes, tt[:, :span], contract, preferred_element_type=jnp.float32)
        for doc in range(DOC_COUNT):
            rows = doc_rows[doc] & (lead != doc)
            y = y + jnp.where(rows, local[doc * blocks : (doc + 1) * blocks], 0.0)
        y = y + bias_ref[channel] * xf
        y_ref[k] = y.astype(y_ref.dtype)


def pallas_conv(x_cm, f_cm, doc_ids, bias_cm):
    chans, seq = x_cm.shape
    span = SPAN
    blocks = seq // span
    step = CHANNELS_PER_STEP
    xb = x_cm.reshape(chans, blocks, span)[:, :, ::-1]
    docb = doc_ids.reshape(blocks, span)
    starts = jnp.sum(doc_ids[None, :] < docb[:, :1], axis=1)
    lag = lax.broadcasted_iota(jnp.int32, (blocks, blocks, span), 1)
    tgt = lax.broadcasted_iota(jnp.int32, (blocks, blocks, span), 0)
    off = span - 1 - lax.broadcasted_iota(jnp.int32, (blocks, blocks, span), 2)
    mask = (tgt >= lag) & (span * (tgt - lag) + off >= starts[:, None, None])
    mask = mask.astype(jnp.float32).reshape(blocks, seq)
    out = pl.pallas_call(
        conv_kernel,
        grid=(chans // step,),
        in_specs=[
            pl.BlockSpec(memory_space=pltpu.SMEM),
            pl.BlockSpec((step, 1, seq), lambda c: (c, 0, 0)),
            pl.BlockSpec((step, blocks, span), lambda c: (c, 0, 0)),
            pl.BlockSpec((blocks, span), lambda c: (0, 0)),
            pl.BlockSpec((blocks, seq), lambda c: (0, 0)),
        ],
        out_specs=pl.BlockSpec((step, blocks, span), lambda c: (c, 0, 0)),
        out_shape=jax.ShapeDtypeStruct((chans, blocks, span), jnp.bfloat16),
    )(bias_cm, f_cm.reshape(chans, 1, seq), xb, docb[:, ::-1], mask)
    return out[:, :, ::-1]


def body(signal, gate, filt, bias, doc_ids, block_perm, out_weight):
    span = SPAN
    rows, chans = signal.shape
    blocks = block_perm.shape[0]
    seq = blocks * span
    n_ctx = seq // rows
    per_dev = chans // n_ctx
    ctx_index = lax.axis_index("ctx")

    inverse = jnp.zeros((blocks,), jnp.int32).at[block_perm].set(jnp.arange(blocks, dtype=jnp.int32))

    def slots_to_natural(a):
        return jnp.take(a.reshape(per_dev, blocks, span), inverse, axis=1).reshape(per_dev, seq)

    packed = jnp.stack(
        [a.reshape(rows, n_ctx, per_dev) for a in (signal, filt)], axis=2
    ).reshape(rows, n_ctx * 2 * per_dev)
    arrived = lax.all_to_all(packed, "ctx", 1, 0, tiled=True).T
    x_cm = slots_to_natural(arrived[:per_dev])
    f_cm = arrived[per_dev:]
    bias_cm = lax.dynamic_slice_in_dim(bias, ctx_index * per_dev, per_dev)
    pre = pallas_conv(x_cm, f_cm, doc_ids, bias_cm)
    pre_slots = jnp.take(pre, block_perm, axis=1)
    pre_slots = pre_slots.reshape(per_dev, seq).T
    pre_local = lax.all_to_all(pre_slots, "ctx", 0, 1, tiled=True)
    gated_local = (gate.astype(jnp.float32) * pre_local.astype(jnp.float32)).astype(jnp.bfloat16)
    n_tp = out_weight.shape[1] // chans
    partial_value = jnp.dot(gated_local, out_weight, preferred_element_type=jnp.float32)
    parts = lax.all_to_all(
        partial_value.astype(jnp.bfloat16).reshape(rows, n_tp, chans), "tp", 1, 1, tiled=True
    )
    return jnp.sum(parts.astype(jnp.float32), axis=1).astype(jnp.bfloat16)


def solution(mesh):
    return jax.shard_map(
        body,
        mesh=mesh,
        in_specs=(P("ctx", "tp"), P("ctx", "tp"), P("ctx", "tp"), P("tp"), P(), P(), P("tp", None)),
        out_specs=P("ctx", "tp"),
        check_vma=False,
    )
```

```python
import jax
import jax.numpy as jnp
from jax import lax
from jax.experimental import pallas as pl
from jax.experimental.pallas import tpu as pltpu
from jax.sharding import PartitionSpec as P

SPAN = 64
DOC_COUNT = 4


CHANNELS_PER_STEP = 8


def conv_kernel(base_ref, bias_ref, f_ref, x_ref, doc_ref, mask_ref, y_ref):
    blocks, span = x_ref.shape[1], x_ref.shape[2]
    seq = blocks * span
    lanes = 2 * span
    docs = doc_ref[...]
    lead = docs[:, span - 1 : span]
    lead_rows = docs == lead
    doc_rows = [docs == doc for doc in range(DOC_COUNT)]
    contract = (((1,), (1,)), ((), ()))
    for k in range(x_ref.shape[0]):
        channel = pl.program_id(0) * x_ref.shape[0] + k
        frow = f_ref[k].astype(jnp.float32)
        frow = jnp.concatenate([frow, jnp.zeros((1, lanes), jnp.float32)], axis=1)
        fb = jnp.broadcast_to(frow, (span, seq + lanes))
        tt = pltpu.roll(fb, 0, 1, stride=1, stride_axis=0)[:, :seq].astype(jnp.bfloat16)
        x = x_ref[k]
        xf = x.astype(jnp.float32)
        pair = jnp.concatenate([xf, pltpu.roll(xf, 1, 0)], axis=1)
        src = jnp.concatenate(
            [pair] + [pltpu.roll(pair, 2 * p, 0) for p in range(1, seq // lanes)], axis=1
        )
        src = (src * mask_ref[...]).astype(jnp.bfloat16)
        y = lax.dot_general(src, tt, contract, preferred_element_type=jnp.float32)
        y = jnp.where(lead_rows, y, 0.0)
        zero = jnp.zeros_like(x)
        planes = jnp.concatenate([jnp.where(rows, x, zero) for rows in doc_rows], axis=0)
        local = lax.dot_general(planes, tt[:, :span], contract, preferred_element_type=jnp.float32)
        for doc in range(DOC_COUNT):
            rows = doc_rows[doc] & (lead != doc)
            y = y + jnp.where(rows, local[doc * blocks : (doc + 1) * blocks], 0.0)
        y = y + bias_ref[base_ref[0] + channel] * xf
        y_ref[k] = y.astype(y_ref.dtype)


def pallas_conv(x_cm, f_cm, doc_ids, bias, base):
    chans, seq = x_cm.shape
    span = SPAN
    blocks = seq // span
    step = CHANNELS_PER_STEP
    xb = x_cm.reshape(chans, blocks, span)[:, :, ::-1]
    docb = doc_ids.reshape(blocks, span)
    starts = jnp.sum(doc_ids[None, :] < docb[:, :1], axis=1)
    lag = lax.broadcasted_iota(jnp.int32, (blocks, blocks, span), 1)
    tgt = lax.broadcasted_iota(jnp.int32, (blocks, blocks, span), 0)
    off = span - 1 - lax.broadcasted_iota(jnp.int32, (blocks, blocks, span), 2)
    mask = (tgt >= lag) & (span * (tgt - lag) + off >= starts[:, None, None])
    mask = mask.astype(jnp.float32).reshape(blocks, seq)
    out = pl.pallas_call(
        conv_kernel,
        grid=(chans // step,),
        in_specs=[
            pl.BlockSpec(memory_space=pltpu.SMEM),
            pl.BlockSpec(memory_space=pltpu.SMEM),
            pl.BlockSpec((step, 1, seq), lambda c: (c, 0, 0)),
            pl.BlockSpec((step, blocks, span), lambda c: (c, 0, 0)),
            pl.BlockSpec((blocks, span), lambda c: (0, 0)),
            pl.BlockSpec((blocks, seq), lambda c: (0, 0)),
        ],
        out_specs=pl.BlockSpec((step, blocks, span), lambda c: (c, 0, 0)),
        out_shape=jax.ShapeDtypeStruct((chans, blocks, span), jnp.bfloat16),
    )(base, bias, f_cm.reshape(chans, 1, seq), xb, docb[:, ::-1], mask)
    return out[:, :, ::-1]


def body(signal, gate, filt, bias, doc_ids, block_perm, out_weight):
    span = SPAN
    rows, chans = signal.shape
    blocks = block_perm.shape[0]
    seq = blocks * span
    n_ctx = seq // rows
    per_dev = chans // n_ctx
    ctx_index = lax.axis_index("ctx")

    inverse = jnp.zeros((blocks,), jnp.int32).at[block_perm].set(jnp.arange(blocks, dtype=jnp.int32))

    def slots_to_natural(a):
        return jnp.take(a.reshape(per_dev, blocks, span), inverse, axis=1).reshape(per_dev, seq)

    packed = jnp.stack(
        [a.reshape(rows, n_ctx, per_dev) for a in (signal, filt)], axis=2
    ).reshape(rows, n_ctx * 2 * per_dev)
    arrived = lax.all_to_all(packed, "ctx", 1, 0, tiled=True).T
    x_cm = slots_to_natural(arrived[:per_dev])
    f_cm = arrived[per_dev:]
    pre = pallas_conv(x_cm, f_cm, doc_ids, bias, (ctx_index * per_dev).reshape(1))
    pre_slots = jnp.take(pre, block_perm, axis=1)
    pre_slots = pre_slots.reshape(per_dev, seq).T
    pre_local = lax.all_to_all(pre_slots, "ctx", 0, 1, tiled=True)
    gated_local = (gate.astype(jnp.float32) * pre_local.astype(jnp.float32)).astype(jnp.bfloat16)
    tp_index = lax.axis_index("tp")
    n_tp = out_weight.shape[1] // chans
    total = None
    for offset in range(n_tp):
        target = (tp_index + offset) % n_tp
        w_cols = lax.dynamic_slice_in_dim(out_weight, target * chans, chans, axis=1)
        part = jnp.dot(gated_local, w_cols, preferred_element_type=jnp.float32)
        if offset:
            pairs = [(i, (i + offset) % n_tp) for i in range(n_tp)]
            part = lax.ppermute(part.astype(jnp.bfloat16), "tp", pairs).astype(jnp.float32)
        total = part if total is None else total + part
    return total.astype(jnp.bfloat16)


def solution(mesh):
    return jax.shard_map(
        body,
        mesh=mesh,
        in_specs=(P("ctx", "tp"), P("ctx", "tp"), P("ctx", "tp"), P("tp"), P(), P(), P("tp", None)),
        out_specs=P("ctx", "tp"),
        check_vma=False,
    )
```

```python
import jax
import jax.numpy as jnp
from jax import lax
from jax.experimental import pallas as pl
from jax.experimental.pallas import tpu as pltpu
from jax.sharding import PartitionSpec as P

SPAN = 64
DOC_COUNT = 4


CHANNELS_PER_STEP = 8


def conv_kernel(base_ref, bias_ref, f_ref, x_ref, doc_ref, mask_ref, y_ref):
    blocks, span = x_ref.shape[1], x_ref.shape[2]
    seq = blocks * span
    lanes = 2 * span
    docs = doc_ref[...]
    lead = docs[:, span - 1 : span]
    lead_rows = docs == lead
    doc_rows = [docs == doc for doc in range(DOC_COUNT)]
    contract = (((1,), (1,)), ((), ()))
    for k in range(x_ref.shape[0]):
        channel = pl.program_id(0) * x_ref.shape[0] + k
        frow = f_ref[k].astype(jnp.float32)
        frow = jnp.concatenate([frow, jnp.zeros((1, lanes), jnp.float32)], axis=1)
        fb = jnp.broadcast_to(frow, (span, seq + lanes))
        tt = pltpu.roll(fb, 0, 1, stride=1, stride_axis=0)[:, :seq].astype(jnp.bfloat16)
        x = x_ref[k]
        xf = x.astype(jnp.float32)
        pair = jnp.concatenate([xf, pltpu.roll(xf, 1, 0)], axis=1)
        src = jnp.concatenate(
            [pair] + [pltpu.roll(pair, 2 * p, 0) for p in range(1, seq // lanes)], axis=1
        )
        src = (src * mask_ref[...]).astype(jnp.bfloat16)
        y = lax.dot_general(src, tt, contract, preferred_element_type=jnp.float32)
        y = jnp.where(lead_rows, y, 0.0)
        zero = jnp.zeros_like(x)
        planes = jnp.concatenate([jnp.where(rows, x, zero) for rows in doc_rows], axis=0)
        local = lax.dot_general(planes, tt[:, :span], contract, preferred_element_type=jnp.float32)
        for doc in range(DOC_COUNT):
            rows = doc_rows[doc] & (lead != doc)
            y = y + jnp.where(rows, local[doc * blocks : (doc + 1) * blocks], 0.0)
        y = y + bias_ref[base_ref[0] + channel] * xf
        y_ref[k] = y.astype(y_ref.dtype)


def pallas_conv(x_rev, f_cm, doc_ids, bias, base):
    chans, blocks, span = x_rev.shape
    seq = blocks * span
    step = CHANNELS_PER_STEP
    xb = x_rev
    docb = doc_ids.reshape(blocks, span)
    starts = jnp.sum(doc_ids[None, :] < docb[:, :1], axis=1)
    lag = lax.broadcasted_iota(jnp.int32, (blocks, blocks, span), 1)
    tgt = lax.broadcasted_iota(jnp.int32, (blocks, blocks, span), 0)
    off = span - 1 - lax.broadcasted_iota(jnp.int32, (blocks, blocks, span), 2)
    mask = (tgt >= lag) & (span * (tgt - lag) + off >= starts[:, None, None])
    mask = mask.astype(jnp.float32).reshape(blocks, seq)
    out = pl.pallas_call(
        conv_kernel,
        grid=(chans // step,),
        in_specs=[
            pl.BlockSpec(memory_space=pltpu.SMEM),
            pl.BlockSpec(memory_space=pltpu.SMEM),
            pl.BlockSpec((step, 1, seq), lambda c: (c, 0, 0)),
            pl.BlockSpec((step, blocks, span), lambda c: (c, 0, 0)),
            pl.BlockSpec((blocks, span), lambda c: (0, 0)),
            pl.BlockSpec((blocks, seq), lambda c: (0, 0)),
        ],
        out_specs=pl.BlockSpec((step, blocks, span), lambda c: (c, 0, 0)),
        out_shape=jax.ShapeDtypeStruct((chans, blocks, span), jnp.bfloat16),
    )(base, bias, f_cm.reshape(chans, 1, seq), xb, docb[:, ::-1], mask)
    return out


def body(signal, gate, filt, bias, doc_ids, block_perm, out_weight):
    span = SPAN
    rows, chans = signal.shape
    blocks = block_perm.shape[0]
    seq = blocks * span
    n_ctx = seq // rows
    per_dev = chans // n_ctx
    ctx_index = lax.axis_index("ctx")

    to_seq = (block_perm[None, :] == jnp.arange(blocks, dtype=jnp.int32)[:, None]).astype(jnp.bfloat16)
    flip = jnp.eye(span, dtype=jnp.bfloat16)[::-1]

    def one_hot(spec, *ops):
        return jnp.einsum(spec, *ops, preferred_element_type=jnp.float32).astype(jnp.bfloat16)

    packed = jnp.stack(
        [a.reshape(rows, n_ctx, per_dev) for a in (signal, filt)], axis=2
    ).reshape(rows, n_ctx * 2 * per_dev)
    arrived = lax.all_to_all(packed, "ctx", 1, 0, tiled=True).T
    x_rev = one_hot("tk,ckm->ctm", to_seq, one_hot("ckj,jm->ckm", arrived[:per_dev].reshape(per_dev, blocks, span), flip))
    f_cm = arrived[per_dev:]
    pre = pallas_conv(x_rev, f_cm, doc_ids, bias, (ctx_index * per_dev).reshape(1))
    pre_slots = one_hot("tk,ctm->ckm", to_seq, one_hot("ctj,jm->ctm", pre, flip))
    pre_slots = pre_slots.reshape(per_dev, seq).T
    pre_local = lax.all_to_all(pre_slots, "ctx", 0, 1, tiled=True)
    gated_local = (gate.astype(jnp.float32) * pre_local.astype(jnp.float32)).astype(jnp.bfloat16)
    tp_index = lax.axis_index("tp")
    n_tp = out_weight.shape[1] // chans
    total = None
    for offset in range(n_tp):
        target = (tp_index + offset) % n_tp
        w_cols = lax.dynamic_slice_in_dim(out_weight, target * chans, chans, axis=1)
        part = jnp.dot(gated_local, w_cols, preferred_element_type=jnp.float32)
        if offset:
            pairs = [(i, (i + offset) % n_tp) for i in range(n_tp)]
            part = lax.ppermute(part.astype(jnp.bfloat16), "tp", pairs).astype(jnp.float32)
        total = part if total is None else total + part
    return total.astype(jnp.bfloat16)


def solution(mesh):
    return jax.shard_map(
        body,
        mesh=mesh,
        in_specs=(P("ctx", "tp"), P("ctx", "tp"), P("ctx", "tp"), P("tp"), P(), P(), P("tp", None)),
        out_specs=P("ctx", "tp"),
        check_vma=False,
    )
```

```python
import jax
import jax.numpy as jnp
from jax import lax
from jax.experimental import pallas as pl
from jax.experimental.pallas import tpu as pltpu
from jax.sharding import PartitionSpec as P

SPAN = 64
DOC_COUNT = 4


CHANNELS_PER_STEP = 8


def conv_kernel(base_ref, bias_ref, f_ref, x_ref, doc_ref, mask_ref, y_ref):
    blocks, span = x_ref.shape[1], x_ref.shape[2]
    seq = blocks * span
    lanes = 2 * span
    docs = doc_ref[...]
    lead = docs[:, span - 1 : span]
    lead_rows = docs == lead
    doc_rows = [docs == doc for doc in range(DOC_COUNT)]
    contract = (((1,), (1,)), ((), ()))
    for k in range(x_ref.shape[0]):
        channel = pl.program_id(0) * x_ref.shape[0] + k
        frow = f_ref[k].astype(jnp.float32)
        frow = jnp.concatenate([frow, jnp.zeros((1, lanes), jnp.float32)], axis=1)
        fb = jnp.broadcast_to(frow, (span, seq + lanes))
        tt = pltpu.roll(fb, 0, 1, stride=1, stride_axis=0)[:, :seq].astype(jnp.bfloat16)
        x = x_ref[k]
        xf = x.astype(jnp.float32)
        pair = jnp.concatenate([xf, pltpu.roll(xf, 1, 0)], axis=1)
        src = jnp.concatenate(
            [pair] + [pltpu.roll(pair, 2 * p, 0) for p in range(1, seq // lanes)], axis=1
        )
        src = (src * mask_ref[...]).astype(jnp.bfloat16)
        y = lax.dot_general(src, tt, contract, preferred_element_type=jnp.float32)
        y = jnp.where(lead_rows, y, 0.0)
        zero = jnp.zeros_like(x)
        planes = jnp.concatenate([jnp.where(rows, x, zero) for rows in doc_rows], axis=0)
        local = lax.dot_general(planes, tt[:, :span], contract, preferred_element_type=jnp.float32)
        for doc in range(DOC_COUNT):
            rows = doc_rows[doc] & (lead != doc)
            y = y + jnp.where(rows, local[doc * blocks : (doc + 1) * blocks], 0.0)
        y = y + bias_ref[base_ref[0] + channel] * xf
        y_ref[k] = y.astype(y_ref.dtype)


def pallas_conv(x_rev, f_cm, doc_ids, bias, base):
    chans, blocks, span = x_rev.shape
    seq = blocks * span
    step = CHANNELS_PER_STEP
    xb = x_rev
    docb = doc_ids.reshape(blocks, span)
    starts = jnp.sum(doc_ids[None, :] < docb[:, :1], axis=1)
    lag = lax.broadcasted_iota(jnp.int32, (blocks, blocks, span), 1)
    tgt = lax.broadcasted_iota(jnp.int32, (blocks, blocks, span), 0)
    off = span - 1 - lax.broadcasted_iota(jnp.int32, (blocks, blocks, span), 2)
    mask = (tgt >= lag) & (span * (tgt - lag) + off >= starts[:, None, None])
    mask = mask.astype(jnp.float32).reshape(blocks, seq)
    out = pl.pallas_call(
        conv_kernel,
        grid=(chans // step,),
        in_specs=[
            pl.BlockSpec(memory_space=pltpu.SMEM),
            pl.BlockSpec(memory_space=pltpu.SMEM),
            pl.BlockSpec((step, 1, seq), lambda c: (c, 0, 0)),
            pl.BlockSpec((step, blocks, span), lambda c: (c, 0, 0)),
            pl.BlockSpec((blocks, span), lambda c: (0, 0)),
            pl.BlockSpec((blocks, seq), lambda c: (0, 0)),
        ],
        out_specs=pl.BlockSpec((step, blocks, span), lambda c: (c, 0, 0)),
        out_shape=jax.ShapeDtypeStruct((chans, blocks, span), jnp.bfloat16),
    )(base, bias, f_cm.reshape(chans, 1, seq), xb, docb[:, ::-1], mask)
    return out


def body(signal, gate, filt, bias, doc_ids, block_perm, out_weight):
    span = SPAN
    rows, chans = signal.shape
    blocks = block_perm.shape[0]
    seq = blocks * span
    n_ctx = seq // rows
    per_dev = chans // n_ctx
    ctx_index = lax.axis_index("ctx")

    to_seq = (block_perm[None, :] == jnp.arange(blocks, dtype=jnp.int32)[:, None]).astype(jnp.bfloat16)
    flip = jnp.eye(span, dtype=jnp.bfloat16)[::-1]

    def one_hot(spec, *ops):
        return jnp.einsum(spec, *ops, preferred_element_type=jnp.float32).astype(jnp.bfloat16)

    packed = jnp.stack(
        [a.reshape(rows, n_ctx, per_dev) for a in (signal, filt)], axis=2
    ).reshape(rows, n_ctx * 2 * per_dev)
    arrived = lax.all_to_all(packed, "ctx", 1, 0, tiled=True).T
    x_rev = one_hot("tk,ckm->ctm", to_seq, one_hot("ckj,jm->ckm", arrived[:per_dev].reshape(per_dev, blocks, span), flip))
    f_cm = arrived[per_dev:]
    pre = pallas_conv(x_rev, f_cm, doc_ids, bias, (ctx_index * per_dev).reshape(1))
    pre_slots = one_hot("tk,ctm->ckm", to_seq, one_hot("ctj,jm->ctm", pre, flip))
    pre_slots = pre_slots.reshape(per_dev, seq).T
    pre_local = lax.all_to_all(pre_slots, "ctx", 0, 1, tiled=True)
    gated_local = (gate.astype(jnp.float32) * pre_local.astype(jnp.float32)).astype(jnp.bfloat16)
    tp_index = lax.axis_index("tp")
    n_tp = out_weight.shape[1] // chans
    high, core = tp_index // 2, tp_index % 2
    w_split = out_weight.reshape(chans, n_tp // 2, 2, chans)
    w_other = lax.dynamic_index_in_dim(w_split, 1 - core, axis=2, keepdims=False)
    p_other = jnp.dot(
        gated_local, w_other.reshape(chans, -1), preferred_element_type=jnp.float32
    )
    recv_core = lax.ppermute(p_other.astype(jnp.bfloat16), "tp", [(i, i ^ 1) for i in range(n_tp)])
    w_mine = lax.dynamic_index_in_dim(w_split, core, axis=2, keepdims=False)
    p_mine = jnp.dot(gated_local, w_mine.reshape(chans, -1), preferred_element_type=jnp.float32)
    p_mine = p_mine + recv_core.astype(jnp.float32)
    send_high = lax.dynamic_slice_in_dim(p_mine, (1 - high) * chans, chans, axis=1)
    keep_high = lax.dynamic_slice_in_dim(p_mine, high * chans, chans, axis=1)
    recv_high = lax.ppermute(
        send_high.astype(jnp.bfloat16), "tp", [(i, i ^ 2) for i in range(n_tp)]
    )
    return (keep_high + recv_high.astype(jnp.float32)).astype(jnp.bfloat16)


def solution(mesh):
    return jax.shard_map(
        body,
        mesh=mesh,
        in_specs=(P("ctx", "tp"), P("ctx", "tp"), P("ctx", "tp"), P("tp"), P(), P(), P("tp", None)),
        out_specs=P("ctx", "tp"),
        check_vma=False,
    )
```

```python
import jax
import jax.numpy as jnp
from jax import lax
from jax.experimental import pallas as pl
from jax.experimental.pallas import tpu as pltpu
from jax.sharding import PartitionSpec as P

SPAN = 64
DOC_COUNT = 4


CHANNELS_PER_STEP = 8


def conv_kernel(base_ref, bias_ref, f_ref, x_ref, doc_ref, mask_ref, y_ref):
    blocks, span = x_ref.shape[1], x_ref.shape[2]
    seq = blocks * span
    lanes = 2 * span
    docs = doc_ref[...]
    lead = docs[:, span - 1 : span]
    lead_rows = docs == lead
    doc_rows = [docs == doc for doc in range(DOC_COUNT)]
    contract = (((1,), (1,)), ((), ()))
    for k in range(x_ref.shape[0]):
        channel = pl.program_id(0) * x_ref.shape[0] + k
        frow = f_ref[k : k + 1, :].astype(jnp.float32)
        frow = jnp.concatenate([frow, jnp.zeros((1, lanes), jnp.float32)], axis=1)
        fb = jnp.broadcast_to(frow, (span, seq + lanes))
        tt = pltpu.roll(fb, 0, 1, stride=1, stride_axis=0)[:, :seq].astype(jnp.bfloat16)
        x = x_ref[k]
        xf = x.astype(jnp.float32)
        pair = jnp.concatenate([xf, pltpu.roll(xf, 1, 0)], axis=1)
        src = jnp.concatenate(
            [pair] + [pltpu.roll(pair, 2 * p, 0) for p in range(1, seq // lanes)], axis=1
        )
        src = (src * mask_ref[...]).astype(jnp.bfloat16)
        y = lax.dot_general(src, tt, contract, preferred_element_type=jnp.float32)
        y = jnp.where(lead_rows, y, 0.0)
        zero = jnp.zeros_like(x)
        planes = jnp.concatenate([jnp.where(rows, x, zero) for rows in doc_rows], axis=0)
        local = lax.dot_general(planes, tt[:, :span], contract, preferred_element_type=jnp.float32)
        for doc in range(DOC_COUNT):
            rows = doc_rows[doc] & (lead != doc)
            y = y + jnp.where(rows, local[doc * blocks : (doc + 1) * blocks], 0.0)
        y = y + bias_ref[base_ref[0] + channel] * xf
        y_ref[k] = y.astype(y_ref.dtype)


def pallas_conv(x_rev, f_cm, doc_ids, bias, base):
    chans, blocks, span = x_rev.shape
    seq = blocks * span
    step = CHANNELS_PER_STEP
    xb = x_rev
    docb = doc_ids.reshape(blocks, span)
    starts = jnp.sum(doc_ids[None, :] < docb[:, :1], axis=1)
    lag = lax.broadcasted_iota(jnp.int32, (blocks, blocks, span), 1)
    tgt = lax.broadcasted_iota(jnp.int32, (blocks, blocks, span), 0)
    off = span - 1 - lax.broadcasted_iota(jnp.int32, (blocks, blocks, span), 2)
    mask = (tgt >= lag) & (span * (tgt - lag) + off >= starts[:, None, None])
    mask = mask.astype(jnp.float32).reshape(blocks, seq)
    out = pl.pallas_call(
        conv_kernel,
        grid=(chans // step,),
        in_specs=[
            pl.BlockSpec(memory_space=pltpu.SMEM),
            pl.BlockSpec(memory_space=pltpu.SMEM),
            pl.BlockSpec((step, seq), lambda c: (c, 0)),
            pl.BlockSpec((step, blocks, span), lambda c: (c, 0, 0)),
            pl.BlockSpec((blocks, span), lambda c: (0, 0)),
            pl.BlockSpec((blocks, seq), lambda c: (0, 0)),
        ],
        out_specs=pl.BlockSpec((step, blocks, span), lambda c: (c, 0, 0)),
        out_shape=jax.ShapeDtypeStruct((chans, blocks, span), jnp.bfloat16),
    )(base, bias, f_cm, xb, docb[:, ::-1], mask)
    return out


def body(signal, gate, filt, bias, doc_ids, block_perm, out_weight):
    span = SPAN
    rows, chans = signal.shape
    blocks = block_perm.shape[0]
    seq = blocks * span
    n_ctx = seq // rows
    per_dev = chans // n_ctx
    ctx_index = lax.axis_index("ctx")

    to_seq = (block_perm[None, :] == jnp.arange(blocks, dtype=jnp.int32)[:, None]).astype(jnp.bfloat16)
    flip = jnp.eye(span, dtype=jnp.bfloat16)[::-1]

    def one_hot(spec, *ops):
        return jnp.einsum(spec, *ops, preferred_element_type=jnp.float32).astype(jnp.bfloat16)

    packed = jnp.stack(
        [a.reshape(rows, n_ctx, per_dev) for a in (signal, filt)], axis=2
    ).reshape(rows, n_ctx * 2 * per_dev)
    arrived = lax.all_to_all(packed, "ctx", 1, 0, tiled=True).T
    x_rev = one_hot("tk,ckm->ctm", to_seq, one_hot("ckj,jm->ckm", arrived[:per_dev].reshape(per_dev, blocks, span), flip))
    f_cm = arrived[per_dev:]
    pre = pallas_conv(x_rev, f_cm, doc_ids, bias, (ctx_index * per_dev).reshape(1))
    pre_slots = one_hot("tk,ctm->ckm", to_seq, one_hot("ctj,jm->ctm", pre, flip))
    pre_slots = pre_slots.reshape(per_dev, seq).T
    pre_local = lax.all_to_all(pre_slots, "ctx", 0, 1, tiled=True)
    gated_local = (gate.astype(jnp.float32) * pre_local.astype(jnp.float32)).astype(jnp.bfloat16)
    tp_index = lax.axis_index("tp")
    n_tp = out_weight.shape[1] // chans
    high, core = tp_index // 2, tp_index % 2
    w_split = out_weight.reshape(chans, n_tp // 2, 2, chans)
    w_other = lax.dynamic_index_in_dim(w_split, 1 - core, axis=2, keepdims=False)
    p_other = jnp.dot(
        gated_local, w_other.reshape(chans, -1), preferred_element_type=jnp.float32
    )
    recv_core = lax.ppermute(p_other.astype(jnp.bfloat16), "tp", [(i, i ^ 1) for i in range(n_tp)])
    w_mine = lax.dynamic_index_in_dim(w_split, core, axis=2, keepdims=False)
    p_mine = jnp.dot(gated_local, w_mine.reshape(chans, -1), preferred_element_type=jnp.float32)
    p_mine = p_mine + recv_core.astype(jnp.float32)
    send_high = lax.dynamic_slice_in_dim(p_mine, (1 - high) * chans, chans, axis=1)
    keep_high = lax.dynamic_slice_in_dim(p_mine, high * chans, chans, axis=1)
    recv_high = lax.ppermute(
        send_high.astype(jnp.bfloat16), "tp", [(i, i ^ 2) for i in range(n_tp)]
    )
    return (keep_high + recv_high.astype(jnp.float32)).astype(jnp.bfloat16)


def solution(mesh):
    return jax.shard_map(
        body,
        mesh=mesh,
        in_specs=(P("ctx", "tp"), P("ctx", "tp"), P("ctx", "tp"), P("tp"), P(), P(), P("tp", None)),
        out_specs=P("ctx", "tp"),
        check_vma=False,
    )
```

```python
import jax
import jax.numpy as jnp
from jax import lax
from jax.experimental import pallas as pl
from jax.experimental.pallas import tpu as pltpu
from jax.sharding import PartitionSpec as P

SPAN = 64
DOC_COUNT = 4


CHANNELS_PER_STEP = 8


def conv_kernel(base_ref, bias_ref, f_ref, x_ref, doc_ref, mask_ref, y_ref):
    blocks, span = x_ref.shape[1], x_ref.shape[2]
    seq = blocks * span
    lanes = 2 * span
    docs = doc_ref[...]
    lead = docs[:, span - 1 : span]
    lead_rows = docs == lead
    doc_rows = [docs == doc for doc in range(DOC_COUNT)]
    contract = (((1,), (1,)), ((), ()))
    for k in range(x_ref.shape[0]):
        channel = pl.program_id(0) * x_ref.shape[0] + k
        frow = f_ref[k : k + 1, :].astype(jnp.float32)
        frow = jnp.concatenate([frow, jnp.zeros((1, lanes), jnp.float32)], axis=1)
        fb = jnp.broadcast_to(frow, (span, seq + lanes))
        tt = pltpu.roll(fb, 0, 1, stride=1, stride_axis=0)[:, :seq].astype(jnp.bfloat16)
        x = x_ref[k]
        xf = x.astype(jnp.float32)
        pair = jnp.concatenate([xf, pltpu.roll(xf, 1, 0)], axis=1).astype(jnp.bfloat16)
        src = jnp.concatenate(
            [pair] + [pltpu.roll(pair, 2 * p, 0) for p in range(1, seq // lanes)], axis=1
        )
        src = src * mask_ref[...]
        y = lax.dot_general(src, tt, contract, preferred_element_type=jnp.float32)
        y = jnp.where(lead_rows, y, 0.0)
        zero = jnp.zeros_like(x)
        planes = jnp.concatenate([jnp.where(rows, x, zero) for rows in doc_rows], axis=0)
        local = lax.dot_general(planes, tt[:, :span], contract, preferred_element_type=jnp.float32)
        for doc in range(DOC_COUNT):
            rows = doc_rows[doc] & (lead != doc)
            y = y + jnp.where(rows, local[doc * blocks : (doc + 1) * blocks], 0.0)
        y = y + bias_ref[base_ref[0] + channel] * xf
        y_ref[k] = y.astype(y_ref.dtype)


def pallas_conv(x_rev, f_cm, doc_ids, bias, base):
    chans, blocks, span = x_rev.shape
    seq = blocks * span
    step = CHANNELS_PER_STEP
    xb = x_rev
    docb = doc_ids.reshape(blocks, span)
    starts = jnp.sum(doc_ids[None, :] < docb[:, :1], axis=1)
    lag = lax.broadcasted_iota(jnp.int32, (blocks, blocks, span), 1)
    tgt = lax.broadcasted_iota(jnp.int32, (blocks, blocks, span), 0)
    off = span - 1 - lax.broadcasted_iota(jnp.int32, (blocks, blocks, span), 2)
    mask = (tgt >= lag) & (span * (tgt - lag) + off >= starts[:, None, None])
    mask = mask.astype(jnp.bfloat16).reshape(blocks, seq)
    out = pl.pallas_call(
        conv_kernel,
        grid=(chans // step,),
        in_specs=[
            pl.BlockSpec(memory_space=pltpu.SMEM),
            pl.BlockSpec(memory_space=pltpu.SMEM),
            pl.BlockSpec((step, seq), lambda c: (c, 0)),
            pl.BlockSpec((step, blocks, span), lambda c: (c, 0, 0)),
            pl.BlockSpec((blocks, span), lambda c: (0, 0)),
            pl.BlockSpec((blocks, seq), lambda c: (0, 0)),
        ],
        out_specs=pl.BlockSpec((step, blocks, span), lambda c: (c, 0, 0)),
        out_shape=jax.ShapeDtypeStruct((chans, blocks, span), jnp.bfloat16),
    )(base, bias, f_cm, xb, docb[:, ::-1], mask)
    return out


def body(signal, gate, filt, bias, doc_ids, block_perm, out_weight):
    span = SPAN
    rows, chans = signal.shape
    blocks = block_perm.shape[0]
    seq = blocks * span
    n_ctx = seq // rows
    per_dev = chans // n_ctx
    ctx_index = lax.axis_index("ctx")

    to_seq = (block_perm[None, :] == jnp.arange(blocks, dtype=jnp.int32)[:, None]).astype(jnp.bfloat16)
    flip = jnp.eye(span, dtype=jnp.bfloat16)[::-1]

    def one_hot(spec, *ops):
        return jnp.einsum(spec, *ops, preferred_element_type=jnp.float32).astype(jnp.bfloat16)

    packed = jnp.stack(
        [a.reshape(rows, n_ctx, per_dev) for a in (signal, filt)], axis=2
    ).reshape(rows, n_ctx * 2 * per_dev)
    arrived = lax.all_to_all(packed, "ctx", 1, 0, tiled=True).T
    x_rev = one_hot("tk,ckm->ctm", to_seq, one_hot("ckj,jm->ckm", arrived[:per_dev].reshape(per_dev, blocks, span), flip))
    f_cm = arrived[per_dev:]
    pre = pallas_conv(x_rev, f_cm, doc_ids, bias, (ctx_index * per_dev).reshape(1))
    pre_slots = one_hot("tk,ctm->ckm", to_seq, one_hot("ctj,jm->ctm", pre, flip))
    pre_slots = pre_slots.reshape(per_dev, seq).T
    pre_local = lax.all_to_all(pre_slots, "ctx", 0, 1, tiled=True)
    gated_local = (gate.astype(jnp.float32) * pre_local.astype(jnp.float32)).astype(jnp.bfloat16)
    tp_index = lax.axis_index("tp")
    n_tp = out_weight.shape[1] // chans
    high, core = tp_index // 2, tp_index % 2
    w_split = out_weight.reshape(chans, n_tp // 2, 2, chans)
    w_other = lax.dynamic_index_in_dim(w_split, 1 - core, axis=2, keepdims=False)
    p_other = jnp.dot(
        gated_local, w_other.reshape(chans, -1), preferred_element_type=jnp.float32
    )
    recv_core = lax.ppermute(p_other.astype(jnp.bfloat16), "tp", [(i, i ^ 1) for i in range(n_tp)])
    w_mine = lax.dynamic_index_in_dim(w_split, core, axis=2, keepdims=False)
    p_mine = jnp.dot(gated_local, w_mine.reshape(chans, -1), preferred_element_type=jnp.float32)
    p_mine = p_mine + recv_core.astype(jnp.float32)
    send_high = lax.dynamic_slice_in_dim(p_mine, (1 - high) * chans, chans, axis=1)
    keep_high = lax.dynamic_slice_in_dim(p_mine, high * chans, chans, axis=1)
    recv_high = lax.ppermute(
        send_high.astype(jnp.bfloat16), "tp", [(i, i ^ 2) for i in range(n_tp)]
    )
    return (keep_high + recv_high.astype(jnp.float32)).astype(jnp.bfloat16)


def solution(mesh):
    return jax.shard_map(
        body,
        mesh=mesh,
        in_specs=(P("ctx", "tp"), P("ctx", "tp"), P("ctx", "tp"), P("tp"), P(), P(), P("tp", None)),
        out_specs=P("ctx", "tp"),
        check_vma=False,
    )
```

```python
import jax
import jax.numpy as jnp
from jax import lax
from jax.experimental import pallas as pl
from jax.experimental.pallas import tpu as pltpu
from jax.sharding import PartitionSpec as P

SPAN = 64
DOC_COUNT = 4


CHANNELS_PER_STEP = 16


def conv_kernel(base_ref, bias_ref, f_ref, x_ref, doc_ref, mask_ref, y_ref):
    blocks, span = x_ref.shape[1], x_ref.shape[2]
    seq = blocks * span
    lanes = 2 * span
    docs = doc_ref[...]
    lead = docs[:, span - 1 : span]
    lead_rows = docs == lead
    doc_rows = [docs == doc for doc in range(DOC_COUNT)]
    contract = (((1,), (1,)), ((), ()))
    for k in range(x_ref.shape[0]):
        channel = pl.program_id(0) * x_ref.shape[0] + k
        frow = f_ref[k : k + 1, :].astype(jnp.float32)
        frow = jnp.concatenate([frow, jnp.zeros((1, lanes), jnp.float32)], axis=1)
        fb = jnp.broadcast_to(frow, (span, seq + lanes))
        tt = pltpu.roll(fb, 0, 1, stride=1, stride_axis=0)[:, :seq].astype(jnp.bfloat16)
        x = x_ref[k]
        xf = x.astype(jnp.float32)
        pair = jnp.concatenate([xf, pltpu.roll(xf, 1, 0)], axis=1)
        src = jnp.concatenate(
            [pair] + [pltpu.roll(pair, 2 * p, 0) for p in range(1, seq // lanes)], axis=1
        )
        src = (src * mask_ref[...]).astype(jnp.bfloat16)
        y = lax.dot_general(src, tt, contract, preferred_element_type=jnp.float32)
        y = jnp.where(lead_rows, y, 0.0)
        zero = jnp.zeros_like(x)
        planes = jnp.concatenate([jnp.where(rows, x, zero) for rows in doc_rows], axis=0)
        local = lax.dot_general(planes, tt[:, :span], contract, preferred_element_type=jnp.float32)
        for doc in range(DOC_COUNT):
            rows = doc_rows[doc] & (lead != doc)
            y = y + jnp.where(rows, local[doc * blocks : (doc + 1) * blocks], 0.0)
        y = y + bias_ref[base_ref[0] + channel] * xf
        y_ref[k] = y.astype(y_ref.dtype)


def pallas_conv(x_rev, f_cm, doc_ids, bias, base):
    chans, blocks, span = x_rev.shape
    seq = blocks * span
    step = CHANNELS_PER_STEP
    xb = x_rev
    docb = doc_ids.reshape(blocks, span)
    starts = jnp.sum(doc_ids[None, :] < docb[:, :1], axis=1)
    lag = lax.broadcasted_iota(jnp.int32, (blocks, blocks, span), 1)
    tgt = lax.broadcasted_iota(jnp.int32, (blocks, blocks, span), 0)
    off = span - 1 - lax.broadcasted_iota(jnp.int32, (blocks, blocks, span), 2)
    mask = (tgt >= lag) & (span * (tgt - lag) + off >= starts[:, None, None])
    mask = mask.astype(jnp.float32).reshape(blocks, seq)
    out = pl.pallas_call(
        conv_kernel,
        grid=(chans // step,),
        in_specs=[
            pl.BlockSpec(memory_space=pltpu.SMEM),
            pl.BlockSpec(memory_space=pltpu.SMEM),
            pl.BlockSpec((step, seq), lambda c: (c, 0)),
            pl.BlockSpec((step, blocks, span), lambda c: (c, 0, 0)),
            pl.BlockSpec((blocks, span), lambda c: (0, 0)),
            pl.BlockSpec((blocks, seq), lambda c: (0, 0)),
        ],
        out_specs=pl.BlockSpec((step, blocks, span), lambda c: (c, 0, 0)),
        out_shape=jax.ShapeDtypeStruct((chans, blocks, span), jnp.bfloat16),
    )(base, bias, f_cm, xb, docb[:, ::-1], mask)
    return out


def body(signal, gate, filt, bias, doc_ids, block_perm, out_weight):
    span = SPAN
    rows, chans = signal.shape
    blocks = block_perm.shape[0]
    seq = blocks * span
    n_ctx = seq // rows
    per_dev = chans // n_ctx
    ctx_index = lax.axis_index("ctx")

    to_seq = (block_perm[None, :] == jnp.arange(blocks, dtype=jnp.int32)[:, None]).astype(jnp.bfloat16)
    flip = jnp.eye(span, dtype=jnp.bfloat16)[::-1]

    def one_hot(spec, *ops):
        return jnp.einsum(spec, *ops, preferred_element_type=jnp.float32).astype(jnp.bfloat16)

    packed = jnp.stack(
        [a.reshape(rows, n_ctx, per_dev) for a in (signal, filt)], axis=2
    ).reshape(rows, n_ctx * 2 * per_dev)
    arrived = lax.all_to_all(packed, "ctx", 1, 0, tiled=True).T
    x_rev = one_hot("tk,ckm->ctm", to_seq, one_hot("ckj,jm->ckm", arrived[:per_dev].reshape(per_dev, blocks, span), flip))
    f_cm = arrived[per_dev:]
    pre = pallas_conv(x_rev, f_cm, doc_ids, bias, (ctx_index * per_dev).reshape(1))
    pre_slots = one_hot("tk,ctm->ckm", to_seq, one_hot("ctj,jm->ctm", pre, flip))
    pre_slots = pre_slots.reshape(per_dev, seq).T
    pre_local = lax.all_to_all(pre_slots, "ctx", 0, 1, tiled=True)
    gated_local = (gate.astype(jnp.float32) * pre_local.astype(jnp.float32)).astype(jnp.bfloat16)
    tp_index = lax.axis_index("tp")
    n_tp = out_weight.shape[1] // chans
    high, core = tp_index // 2, tp_index % 2
    w_split = out_weight.reshape(chans, n_tp // 2, 2, chans)
    w_other = lax.dynamic_index_in_dim(w_split, 1 - core, axis=2, keepdims=False)
    p_other = jnp.dot(
        gated_local, w_other.reshape(chans, -1), preferred_element_type=jnp.float32
    )
    recv_core = lax.ppermute(p_other.astype(jnp.bfloat16), "tp", [(i, i ^ 1) for i in range(n_tp)])
    w_mine = lax.dynamic_index_in_dim(w_split, core, axis=2, keepdims=False)
    p_mine = jnp.dot(gated_local, w_mine.reshape(chans, -1), preferred_element_type=jnp.float32)
    p_mine = p_mine + recv_core.astype(jnp.float32)
    send_high = lax.dynamic_slice_in_dim(p_mine, (1 - high) * chans, chans, axis=1)
    keep_high = lax.dynamic_slice_in_dim(p_mine, high * chans, chans, axis=1)
    recv_high = lax.ppermute(
        send_high.astype(jnp.bfloat16), "tp", [(i, i ^ 2) for i in range(n_tp)]
    )
    return (keep_high + recv_high.astype(jnp.float32)).astype(jnp.bfloat16)


def solution(mesh):
    return jax.shard_map(
        body,
        mesh=mesh,
        in_specs=(P("ctx", "tp"), P("ctx", "tp"), P("ctx", "tp"), P("tp"), P(), P(), P("tp", None)),
        out_specs=P("ctx", "tp"),
        check_vma=False,
    )
```

```python
import jax
import jax.numpy as jnp
from jax import lax
from jax.experimental import pallas as pl
from jax.experimental.pallas import tpu as pltpu
from jax.sharding import PartitionSpec as P

SPAN = 64
DOC_COUNT = 4


CHANNELS_PER_STEP = 8


def conv_kernel(base_ref, bias_ref, f_ref, x_ref, doc_ref, mask_ref, y_ref):
    blocks, span = x_ref.shape[1], x_ref.shape[2]
    seq = blocks * span
    lanes = 2 * span
    docs = doc_ref[...]
    lead = docs[:, span - 1 : span]
    lead_rows = docs == lead
    doc_rows = [docs == doc for doc in range(DOC_COUNT)]
    contract = (((1,), (1,)), ((), ()))
    for k in range(x_ref.shape[0]):
        channel = pl.program_id(0) * x_ref.shape[0] + k
        frow = f_ref[k : k + 1, :].astype(jnp.float32)
        frow = jnp.concatenate([frow, jnp.zeros((1, lanes), jnp.float32)], axis=1)
        fb = jnp.broadcast_to(frow, (span, seq + lanes))
        tt = pltpu.roll(fb, 0, 1, stride=1, stride_axis=0)[:, :seq].astype(jnp.bfloat16)
        x = x_ref[k]
        xf = x.astype(jnp.float32)
        pair = jnp.concatenate([xf, pltpu.roll(xf, 1, 0)], axis=1)
        src = jnp.concatenate(
            [pair] + [pltpu.roll(pair, 2 * p, 0) for p in range(1, seq // lanes)], axis=1
        )
        src = src.astype(jnp.bfloat16) * mask_ref[...]
        y = lax.dot_general(src, tt, contract, preferred_element_type=jnp.float32)
        y = jnp.where(lead_rows, y, 0.0)
        zero = jnp.zeros_like(x)
        planes = jnp.concatenate([jnp.where(rows, x, zero) for rows in doc_rows], axis=0)
        local = lax.dot_general(planes, tt[:, :span], contract, preferred_element_type=jnp.float32)
        for doc in range(DOC_COUNT):
            rows = doc_rows[doc] & (lead != doc)
            y = y + jnp.where(rows, local[doc * blocks : (doc + 1) * blocks], 0.0)
        y = y + bias_ref[base_ref[0] + channel] * xf
        y_ref[k] = y.astype(y_ref.dtype)


def pallas_conv(x_rev, f_cm, doc_ids, bias, base):
    chans, blocks, span = x_rev.shape
    seq = blocks * span
    step = CHANNELS_PER_STEP
    xb = x_rev
    docb = doc_ids.reshape(blocks, span)
    starts = jnp.sum(doc_ids[None, :] < docb[:, :1], axis=1)
    lag = lax.broadcasted_iota(jnp.int32, (blocks, blocks, span), 1)
    tgt = lax.broadcasted_iota(jnp.int32, (blocks, blocks, span), 0)
    off = span - 1 - lax.broadcasted_iota(jnp.int32, (blocks, blocks, span), 2)
    mask = (tgt >= lag) & (span * (tgt - lag) + off >= starts[:, None, None])
    mask = mask.astype(jnp.bfloat16).reshape(blocks, seq)
    out = pl.pallas_call(
        conv_kernel,
        grid=(chans // step,),
        in_specs=[
            pl.BlockSpec(memory_space=pltpu.SMEM),
            pl.BlockSpec(memory_space=pltpu.SMEM),
            pl.BlockSpec((step, seq), lambda c: (c, 0)),
            pl.BlockSpec((step, blocks, span), lambda c: (c, 0, 0)),
            pl.BlockSpec((blocks, span), lambda c: (0, 0)),
            pl.BlockSpec((blocks, seq), lambda c: (0, 0)),
        ],
        out_specs=pl.BlockSpec((step, blocks, span), lambda c: (c, 0, 0)),
        out_shape=jax.ShapeDtypeStruct((chans, blocks, span), jnp.bfloat16),
    )(base, bias, f_cm, xb, docb[:, ::-1], mask)
    return out


def body(signal, gate, filt, bias, doc_ids, block_perm, out_weight):
    span = SPAN
    rows, chans = signal.shape
    blocks = block_perm.shape[0]
    seq = blocks * span
    n_ctx = seq // rows
    per_dev = chans // n_ctx
    ctx_index = lax.axis_index("ctx")

    to_seq = (block_perm[None, :] == jnp.arange(blocks, dtype=jnp.int32)[:, None]).astype(jnp.bfloat16)
    flip = jnp.eye(span, dtype=jnp.bfloat16)[::-1]

    def one_hot(spec, *ops):
        return jnp.einsum(spec, *ops, preferred_element_type=jnp.float32).astype(jnp.bfloat16)

    packed = jnp.stack(
        [a.reshape(rows, n_ctx, per_dev) for a in (signal, filt)], axis=2
    ).reshape(rows, n_ctx * 2 * per_dev)
    arrived = lax.all_to_all(packed, "ctx", 1, 0, tiled=True).T
    x_rev = one_hot("tk,ckm->ctm", to_seq, one_hot("ckj,jm->ckm", arrived[:per_dev].reshape(per_dev, blocks, span), flip))
    f_cm = arrived[per_dev:]
    pre = pallas_conv(x_rev, f_cm, doc_ids, bias, (ctx_index * per_dev).reshape(1))
    pre_slots = one_hot("tk,ctm->ckm", to_seq, one_hot("ctj,jm->ctm", pre, flip))
    pre_slots = pre_slots.reshape(per_dev, seq).T
    pre_local = lax.all_to_all(pre_slots, "ctx", 0, 1, tiled=True)
    gated_local = (gate.astype(jnp.float32) * pre_local.astype(jnp.float32)).astype(jnp.bfloat16)
    tp_index = lax.axis_index("tp")
    n_tp = out_weight.shape[1] // chans
    high, core = tp_index // 2, tp_index % 2
    w_split = out_weight.reshape(chans, n_tp // 2, 2, chans)
    w_other = lax.dynamic_index_in_dim(w_split, 1 - core, axis=2, keepdims=False)
    p_other = jnp.dot(
        gated_local, w_other.reshape(chans, -1), preferred_element_type=jnp.float32
    )
    recv_core = lax.ppermute(p_other.astype(jnp.bfloat16), "tp", [(i, i ^ 1) for i in range(n_tp)])
    w_mine = lax.dynamic_index_in_dim(w_split, core, axis=2, keepdims=False)
    p_mine = jnp.dot(gated_local, w_mine.reshape(chans, -1), preferred_element_type=jnp.float32)
    p_mine = p_mine + recv_core.astype(jnp.float32)
    send_high = lax.dynamic_slice_in_dim(p_mine, (1 - high) * chans, chans, axis=1)
    keep_high = lax.dynamic_slice_in_dim(p_mine, high * chans, chans, axis=1)
    recv_high = lax.ppermute(
        send_high.astype(jnp.bfloat16), "tp", [(i, i ^ 2) for i in range(n_tp)]
    )
    return (keep_high + recv_high.astype(jnp.float32)).astype(jnp.bfloat16)


def solution(mesh):
    return jax.shard_map(
        body,
        mesh=mesh,
        in_specs=(P("ctx", "tp"), P("ctx", "tp"), P("ctx", "tp"), P("tp"), P(), P(), P("tp", None)),
        out_specs=P("ctx", "tp"),
        check_vma=False,
    )
```

```python
import jax
import jax.numpy as jnp
from jax import lax
from jax.experimental import pallas as pl
from jax.experimental.pallas import tpu as pltpu
from jax.sharding import PartitionSpec as P

SPAN = 64
DOC_COUNT = 4


CHANNELS_PER_STEP = 8


def conv_kernel(base_ref, bias_ref, f_ref, x_ref, doc_ref, mask_ref, y_ref):
    blocks, span = x_ref.shape[1], x_ref.shape[2]
    seq = blocks * span
    lanes = 2 * span
    docs = doc_ref[...]
    lead = docs[:, span - 1 : span]
    lead_rows = docs == lead
    doc_rows = [docs == doc for doc in range(DOC_COUNT)]
    contract = (((1,), (1,)), ((), ()))
    for k in range(x_ref.shape[0]):
        channel = pl.program_id(0) * x_ref.shape[0] + k
        frow = f_ref[k : k + 1, :].astype(jnp.float32)
        frow = jnp.concatenate([frow, jnp.zeros((1, lanes), jnp.float32)], axis=1)
        fb = jnp.broadcast_to(frow, (span, seq + lanes))
        tt = pltpu.roll(fb, 0, 1, stride=1, stride_axis=0)[:, :seq].astype(jnp.bfloat16)
        x = x_ref[k]
        xf = x.astype(jnp.float32)
        pair = jnp.concatenate([xf, pltpu.roll(xf, 1, 0)], axis=1)
        src = jnp.concatenate(
            [pair] + [pltpu.roll(pair, 2 * p, 0) for p in range(1, seq // lanes)], axis=1
        )
        src = (src * mask_ref[...]).astype(jnp.bfloat16)
        y = lax.dot_general(src, tt, contract, preferred_element_type=jnp.float32)
        y = jnp.where(lead_rows, y, 0.0)
        zero = jnp.zeros_like(x)
        planes = jnp.concatenate([jnp.where(rows, x, zero) for rows in doc_rows], axis=0)
        local = lax.dot_general(planes, tt[:, :span], contract, preferred_element_type=jnp.float32)
        for doc in range(DOC_COUNT):
            rows = doc_rows[doc] & (lead != doc)
            y = y + jnp.where(rows, local[doc * blocks : (doc + 1) * blocks], 0.0)
        y = y + bias_ref[base_ref[0] + channel] * xf
        y_ref[k] = y.astype(y_ref.dtype)


def pallas_conv(x_rev, f_cm, doc_ids, bias, base):
    chans, blocks, span = x_rev.shape
    seq = blocks * span
    step = CHANNELS_PER_STEP
    xb = x_rev
    docb = doc_ids.reshape(blocks, span)
    starts = jnp.sum(doc_ids[None, :] < docb[:, :1], axis=1)
    lag = lax.broadcasted_iota(jnp.int32, (blocks, blocks, span), 1)
    tgt = lax.broadcasted_iota(jnp.int32, (blocks, blocks, span), 0)
    off = span - 1 - lax.broadcasted_iota(jnp.int32, (blocks, blocks, span), 2)
    mask = (tgt >= lag) & (span * (tgt - lag) + off >= starts[:, None, None])
    mask = mask.astype(jnp.float32).reshape(blocks, seq)
    out = pl.pallas_call(
        conv_kernel,
        grid=(chans // step,),
        in_specs=[
            pl.BlockSpec(memory_space=pltpu.SMEM),
            pl.BlockSpec(memory_space=pltpu.SMEM),
            pl.BlockSpec((step, seq), lambda c: (c, 0)),
            pl.BlockSpec((step, blocks, span), lambda c: (c, 0, 0)),
            pl.BlockSpec((blocks, span), lambda c: (0, 0)),
            pl.BlockSpec((blocks, seq), lambda c: (0, 0)),
        ],
        out_specs=pl.BlockSpec((step, blocks, span), lambda c: (c, 0, 0)),
        out_shape=jax.ShapeDtypeStruct((chans, blocks, span), jnp.bfloat16),
    )(base, bias, f_cm, xb, docb[:, ::-1], mask)
    return out


def body(signal, gate, filt, bias, doc_ids, block_perm, out_weight):
    span = SPAN
    rows, chans = signal.shape
    blocks = block_perm.shape[0]
    seq = blocks * span
    n_ctx = seq // rows
    per_dev = chans // n_ctx
    ctx_index = lax.axis_index("ctx")

    to_seq = (block_perm[None, :] == jnp.arange(blocks, dtype=jnp.int32)[:, None]).astype(jnp.bfloat16)
    flip = jnp.eye(span, dtype=jnp.bfloat16)[::-1]

    def one_hot(spec, *ops):
        return jnp.einsum(spec, *ops, preferred_element_type=jnp.float32).astype(jnp.bfloat16)

    packed = jnp.stack(
        [a.reshape(rows, n_ctx, per_dev) for a in (signal, filt)], axis=2
    ).reshape(rows, n_ctx * 2 * per_dev)
    arrived = lax.all_to_all(packed, "ctx", 1, 0, tiled=True).T
    x_rev = one_hot("tk,ckm->ctm", to_seq, one_hot("ckj,jm->ckm", arrived[:per_dev].reshape(per_dev, blocks, span), flip))
    f_cm = arrived[per_dev:]
    pre = pallas_conv(x_rev, f_cm, doc_ids, bias, (ctx_index * per_dev).reshape(1))
    pre_slots = one_hot("tk,ctm->ckm", to_seq, one_hot("ctj,jm->ctm", pre, flip))
    pre_slots = pre_slots.reshape(per_dev, seq).T
    pre_local = lax.all_to_all(pre_slots, "ctx", 0, 1, tiled=True)
    gated_local = (gate.astype(jnp.float32) * pre_local.astype(jnp.float32)).astype(jnp.bfloat16)
    tp_index = lax.axis_index("tp")
    n_tp = out_weight.shape[1] // chans
    high, core = tp_index // 2, tp_index % 2
    half = out_weight.shape[1] // 2
    w_other = lax.dynamic_slice_in_dim(out_weight, (1 - high) * half, half, axis=1)
    p_other = jnp.dot(gated_local, w_other, preferred_element_type=jnp.float32)
    recv_high = lax.ppermute(p_other.astype(jnp.bfloat16), "tp", [(i, i ^ 2) for i in range(n_tp)])
    w_mine = lax.dynamic_slice_in_dim(out_weight, high * half, half, axis=1)
    p_mine = jnp.dot(gated_local, w_mine, preferred_element_type=jnp.float32)
    p_mine = p_mine + recv_high.astype(jnp.float32)
    send_core = lax.dynamic_slice_in_dim(p_mine, (1 - core) * chans, chans, axis=1)
    keep_core = lax.dynamic_slice_in_dim(p_mine, core * chans, chans, axis=1)
    recv_core = lax.ppermute(send_core.astype(jnp.bfloat16), "tp", [(i, i ^ 1) for i in range(n_tp)])
    return (keep_core + recv_core.astype(jnp.float32)).astype(jnp.bfloat16)


def solution(mesh):
    return jax.shard_map(
        body,
        mesh=mesh,
        in_specs=(P("ctx", "tp"), P("ctx", "tp"), P("ctx", "tp"), P("tp"), P(), P(), P("tp", None)),
        out_specs=P("ctx", "tp"),
        check_vma=False,
    )
```
